32 devices in a mesh: seq: 8 (over z, x), qry: 4 (over y, core).
Axes of the slice: x: 2, y: 2, z: 4, core: 2. Of those that a mesh axis runs over, the one named last changes fastest.
Arguments:
- context_in: bfloat16 [8, 512, 768], P('seq'), may hold values from -6 to 6
- query_in: bfloat16 [8, 1024, 768], P('seq', 'qry'), may hold values from -6 to 6
- context_seg: int32 [8, 512], P('seq'), may hold values from 0 to 7, never falling along the last dimension, each value on 1 to 128 neighbouring positions
- query_seg: int32 [8, 1024], P('seq', 'qry'), may hold values from 0 to 7
- attn_gain: bfloat16 [768], replicated, may hold values from 0.25 to 1.75
- attn_shift: bfloat16 [768], replicated, may hold values from -3 to 3
- w_query: bfloat16 [768, 768], replicated, may hold values from -0.21875 to 0.21875
- b_query: bfloat16 [768], replicated, may hold values from -4 to 4
- w_key: bfloat16 [768, 768], replicated, may hold values from -0.21875 to 0.21875
- w_value: bfloat16 [768, 768], replicated, may hold values from -0.21875 to 0.21875
- b_value: bfloat16 [768], replicated, may hold values from -4 to 4
- w_out: bfloat16 [768, 768], replicated, may hold values from -0.875 to 0.875
- b_out: bfloat16 [768], replicated, may hold values from -4 to 4
- mlp_gain: bfloat16 [768], replicated, may hold values from 0.25 to 1.75
- mlp_shift: bfloat16 [768], replicated, may hold values from -3 to 3
- w_in: bfloat16 [768, 3072], replicated, may hold values from -0.21875 to 0.21875
- b_in: bfloat16 [3072], replicated, may hold values from -4 to 4
- w_down: bfloat16 [3072, 768], replicated, may hold values from -0.109375 to 0.109375
- b_down: bfloat16 [768], replicated, may hold values from -4 to 4
- context_cot: bfloat16 [8, 512, 768], P('seq'), may hold values from -6 to 6
- query_cot: bfloat16 [8, 1024, 768], P('seq', 'qry'), may hold values from -6 to 6
Outputs:
- context_out: bfloat16 [8, 512, 768], P('seq')
- query_out: bfloat16 [8, 1024, 768], P('seq', 'qry')
- context_grad: float32 [8, 512, 768], P('seq')
- query_grad: float32 [8, 1024, 768], P('seq', 'qry')
- grad_attn_gain: float32 [768], replicated
- grad_attn_shift: float32 [768], replicated
- grad_w_query: float32 [768, 768], P('seq', 'qry')
- grad_b_query: float32 [768], replicated
- grad_w_key: float32 [768, 768], P('seq', 'qry')
- grad_w_value: float32 [768, 768], P('seq', 'qry')
- grad_b_value: float32 [768], replicated
- grad_w_out: float32 [768, 768], P('seq', 'qry')
- grad_b_out: float32 [768], replicated
- grad_mlp_gain: float32 [768], replicated
- grad_mlp_shift: float32 [768], replicated
- grad_w_in: float32 [768, 3072], P('seq', 'qry')
- grad_b_in: float32 [3072], replicated
- grad_w_down: float32 [3072, 768], P('seq', 'qry')
- grad_b_down: float32 [768], replicated
The draws below stay inside these ranges and needn't reach their ends.
Inputs may be any that keep to these rules, and one draw needn't show every extreme that they name: `context_seg`: in each sequence the context rows' table ids never fall, every table 0 to 7 has 1 to 128 context rows, and one has exactly 128. `query_seg`: table id of each query row, in any order.
All inputs are finite; a program needn't handle non-finite values.
Results may differ from the reference program's by a relative error of at most 0.012.
Values sent between devices are 32-bit elements; how exact they have to be, the bound alone decides.
No kernel may reach another device: no remote copies, remote signals or barrier semaphores. Data moves between devices by JAX's collectives and lax.ppermute only.
A program may use at most 192 MiB of HBM per device.

```python
import math
import jax
import jax.numpy as jnp
import numpy as np
from jax import lax

D = 768
HEADS = 12
HEAD_DIM = 64
FF = 3072
CTX = 512
TABLES = 8
MOST = 128
QRY = 1024
SEQS = 8


def set_ends(drawn, stream_key, least, high):
    longest = drawn.shape.index(max(drawn.shape))
    spots = []
    for shift in (0, 1):
        where = [jax.random.randint(jax.random.fold_in(stream_key, axis), (), 0, length) for axis, length in enumerate(drawn.shape)]
        where[longest] = (where[longest] + shift) % drawn.shape[longest]
        spots.append(tuple(where))
    return drawn.at[spots[0]].set(least).at[spots[1]].set(high)


def block_levels(key, shape, split, least, high):
    level, own = 1.0, jax.random.fold_in(key, 6)
    for axis_at, blocks in split:
        draws = jnp.exp(jax.random.uniform(jax.random.fold_in(own, axis_at), (blocks,), jnp.float32, least / len(split), high / len(split)))
        level = level * jnp.repeat(draws, shape[axis_at] // blocks).reshape([-1 if axis == axis_at else 1 for axis in range(len(shape))])
    return level


def length_profile(number_of, total, most, lean):
    loads = [(1 << 20) // math.isqrt(standing ** lean) + 1 for standing in range(2, number_of + 1)]
    spare, given = total - most - (number_of - 1), [1] * (number_of - 1)
    while spare > 0:
        movable = [i for i in range(number_of - 1) if given[i] < most]
        whole, remaining = sum([loads[i] for i in movable]), spare
        for i in movable:
            more = min(most - given[i], max(1, remaining * loads[i] // whole), spare)
            given[i] = given[i] + more
            spare = spare - more
    return np.array([most] + given)


def uneven(stream_key, amount, total, limit, slope):
    if amount == 2:
        one = jax.random.randint(stream_key, (), max(1, total - limit), min(limit, total - 1) + 1)
        return jnp.stack([one, total - one])
    tallies = jnp.asarray(length_profile(amount, total, limit, slope), jnp.int32)
    pairs = (amount - 1) // 2
    source_of, sink = tallies[1:1 + 2 * pairs:2], tallies[2:2 + 2 * pairs:2]
    room = jnp.minimum(source_of - 1, limit - sink)
    passed = jax.random.randint(jax.random.fold_in(stream_key, 1), (pairs,), 0, 1 << 20) % (room + 1)
    tallies = tallies.at[1:1 + 2 * pairs:2].set(source_of - passed).at[2:2 + 2 * pairs:2].set(sink + passed)
    return tallies[jax.random.permutation(jax.random.fold_in(stream_key, 2), amount)]


def centred(key, extent, deviation, most, split=(), kind=jnp.bfloat16):
    entries = jax.random.normal(key, extent, jnp.float32) * deviation
    if len(split) > 0:
        entries = block_levels(key, extent, split, -0.22, 0.18) * entries
    return jnp.clip(entries, min=-most, max=most).astype(kind)


def setup_inputs(seed: int = 0) -> dict:
    keys = jax.random.split(jax.random.key(seed), 22)
    return {
        "context_in": centred(keys[0], (SEQS, CTX, D), 1.0, 6.0, ((0, 8),)),
        "query_in": centred(keys[1], (SEQS, QRY, D), 1.0, 6.0, ((0, 8), (1, 4))),
        "context_seg": jax.vmap(lambda own: jnp.searchsorted(jnp.cumsum(uneven(own, TABLES, CTX, MOST, 2)), jnp.arange(CTX), side="right"))(jax.random.split(keys[2], SEQS)).reshape((SEQS, CTX)).astype(jnp.int32),
        "query_seg": set_ends(jax.random.randint(keys[3], (SEQS, QRY), 0, TABLES), jax.random.fold_in(keys[3], 1), 0, TABLES - 1).astype(jnp.int32),
        "attn_gain": jnp.clip(1.0 + 0.15 * jax.random.normal(keys[4], (D,), jnp.float32), 0.25, 1.75).astype(jnp.bfloat16),
        "attn_shift": centred(keys[5], (D,), 0.3, 3.0),
        "w_query": centred(keys[6], (D, D), D ** -0.5, 0.21875),
        "b_query": centred(keys[7], (D,), 0.5, 4.0),
        "w_key": centred(keys[8], (D, D), D ** -0.5, 0.21875),
        "w_value": centred(keys[9], (D, D), D ** -0.5, 0.21875),
        "b_value": centred(keys[10], (D,), 0.5, 4.0),
        "w_out": centred(keys[11], (D, D), (D // 16) ** -0.5, 0.875),
        "b_out": centred(keys[12], (D,), 0.5, 4.0),
        "mlp_gain": jnp.clip(1.0 + 0.15 * jax.random.normal(keys[13], (D,), jnp.float32), 0.25, 1.75).astype(jnp.bfloat16),
        "mlp_shift": centred(keys[14], (D,), 0.3, 3.0),
        "w_in": centred(keys[15], (D, FF), D ** -0.5, 0.21875),
        "b_in": centred(keys[16], (FF,), 0.5, 4.0),
        "w_down": centred(keys[17], (FF, D), FF ** -0.5, 0.109375),
        "b_down": centred(keys[18], (D,), 0.5, 4.0),
        "context_cot": centred(keys[19], (SEQS, CTX, D), 1.0, 6.0, ((0, 8),)),
        "query_cot": centred(keys[20], (SEQS, QRY, D), 1.0, 6.0, ((0, 8), (1, 4))),
    }


EPSILON = 1e-05
MASKED = -1e+30
HIGHEST = lax.Precision.HIGHEST

@jax.custom_vjp
def low(v):
    return lax.optimization_barrier(v.astype(jnp.bfloat16)).astype(jnp.float32)

@jax.custom_vjp
def low_back(v):
    return v

def low_keep(v):
    return (low(v), None)

def low_pass(kept, grad):
    return (grad,)

def back_keep(v):
    return (v, None)

def back_low(kept, grad):
    return (low(grad),)
low.defvjp(low_keep, low_pass)
low_back.defvjp(back_keep, back_low)

def layer_norm(values, gain, offset):
    center = values - lax.optimization_barrier(jnp.mean(values, axis=-1, keepdims=True))
    spread = lax.optimization_barrier(jnp.mean(center * center, axis=-1, keepdims=True))
    return center * lax.rsqrt(spread + EPSILON) * gain + offset

def matmul(left, right):
    return jnp.dot(left, right, precision=HIGHEST)

def split_heads(values):
    return values.reshape(values.shape[0], HEADS, HEAD_DIM)

def one_sequence(params, context, queries, context_seg, query_seg):
    attn_gain, attn_shift, w_query, b_query, w_key, w_value, b_value, w_out, b_out, mlp_gain, mlp_shift, w_in, b_in, w_down, b_down = params
    count = context.shape[0]
    inputs = jnp.concatenate([context, queries], axis=0)
    segments = jnp.concatenate([context_seg, query_seg], axis=0)
    normed_one = low(layer_norm(inputs, attn_gain, attn_shift))
    query_proj = low(low_back(matmul(normed_one, w_query) + b_query))
    key_proj = low(low_back(matmul(normed_one[:count], w_key)))
    value_proj = low(low_back(matmul(normed_one[:count], w_value) + b_value))
    scores = jnp.einsum('rhe,khe->hrk', split_heads(query_proj), split_heads(key_proj), precision=HIGHEST)
    scores = low_back(scores * HEAD_DIM ** (-0.5))
    allowed = (segments[:, None] == context_seg[None, :])[None]
    scores = jnp.where(allowed, scores, MASKED)
    shifted = scores - lax.optimization_barrier(jnp.max(scores, axis=-1, keepdims=True))
    raised = jnp.exp(shifted)
    weights = low(raised / lax.optimization_barrier(jnp.sum(raised, axis=-1, keepdims=True)))
    mixed = jnp.einsum('hrk,khe->rhe', weights, split_heads(value_proj), precision=HIGHEST)
    mixed = low(low_back(mixed.reshape(inputs.shape[0], D)))
    after_attn = inputs + low_back(matmul(mixed, w_out) + b_out)
    normed_two = low(layer_norm(after_attn, mlp_gain, mlp_shift))
    hidden = low(jax.nn.gelu(low_back(matmul(normed_two, w_in) + b_in)))
    result = after_attn + low_back(matmul(hidden, w_down) + b_down)
    return (result[:count], result[count:])

def reference(context_in, query_in, context_seg, query_seg, attn_gain, attn_shift, w_query, b_query, w_key, w_value, b_value, w_out, b_out, mlp_gain, mlp_shift, w_in, b_in, w_down, b_down, context_cot, query_cot):
    params = tuple((item.astype(jnp.float32) for item in (attn_gain, attn_shift, w_query, b_query, w_key, w_value, b_value, w_out, b_out, mlp_gain, mlp_shift, w_in, b_in, w_down, b_down)))

    def forward(weights_all, context_all, queries_all):

        def advance(carry, item):
            context, queries, ctx_ids, qry_ids = item
            paired = jax.checkpoint(one_sequence)(weights_all, context, queries, ctx_ids, qry_ids)
            return (carry, paired)
        _, stacked = lax.scan(advance, jnp.zeros((), jnp.float32), (context_all, queries_all, context_seg, query_seg))
        return stacked
    outputs, pullback = jax.vjp(forward, params, context_in.astype(jnp.float32), query_in.astype(jnp.float32))
    grad_params, context_grad, query_grad = pullback((context_cot.astype(jnp.float32), query_cot.astype(jnp.float32)))
    grad_attn_gain, grad_attn_shift, grad_w_query, grad_b_query, grad_w_key, grad_w_value, grad_b_value, grad_w_out, grad_b_out, grad_mlp_gain, grad_mlp_shift, grad_w_in, grad_b_in, grad_w_down, grad_b_down = grad_params
    return (outputs[0].astype(jnp.bfloat16), outputs[1].astype(jnp.bfloat16), context_grad, query_grad, grad_attn_gain, grad_attn_shift, grad_w_query, grad_b_query, grad_w_key, grad_w_value, grad_b_value, grad_w_out, grad_b_out, grad_mlp_gain, grad_mlp_shift, grad_w_in, grad_b_in, grad_w_down, grad_b_down)
```

```python
import functools

import jax
import jax.numpy as jnp
from jax import lax
from jax.experimental import pallas as pl
from jax.experimental.pallas import tpu as pltpu
from jax.sharding import PartitionSpec as P

D = 768
HEADS = 12
HEAD_DIM = 64
FF = 3072
PAIRS = HEADS // 2

EPSILON = 1e-05
MASKED = -1e30
LOW = jnp.bfloat16
F32 = jnp.float32
SCALING = HEAD_DIM ** (-0.5)
BEND = 0.7978845608028654
CUBE = 0.044715 * BEND


def standardize(values):
    center = values - jnp.mean(values, axis=-1, keepdims=True)
    spread = jnp.mean(center * center, axis=-1, keepdims=True)
    inverse = lax.rsqrt(spread + EPSILON)
    return center * inverse, inverse


def norm_pullback(standard, inverse, gain, grad):
    scaled = grad * gain
    first = jnp.mean(scaled, axis=-1, keepdims=True)
    second = jnp.mean(scaled * standard, axis=-1, keepdims=True)
    return inverse * (scaled - first - standard * second)


def product(left, right):
    return jnp.dot(left, right, preferred_element_type=F32)


def transposed_left(left, right):
    return lax.dot_general(left, right, (((0,), (0,)), ((), ())), preferred_element_type=F32)


def transposed_right(left, right):
    return lax.dot_general(left, right, (((1,), (1,)), ((), ())), preferred_element_type=F32)


def wide(ref):
    return ref[...].astype(F32).reshape(1, -1)


def ds(start, size):
    return pl.ds(pl.multiple_of(start, size), size)


def fold(values):
    return jnp.sum(values.reshape(values.shape[0] // 8, 8, values.shape[1]), axis=0)


def whole(values):
    return jnp.sum(values, axis=0, keepdims=True)


def vmem():
    return pl.BlockSpec(memory_space=pltpu.VMEM)


def hbm():
    return pl.BlockSpec(memory_space=pltpu.HBM)


SMALL = pl.CostEstimate(flops=0, bytes_accessed=0, transcendentals=0)


class Copies:
    def __init__(self, sems):
        self.sems, self.all = sems, []

    def start(self, source, target):
        copy = pltpu.make_async_copy(source, target, self.sems.at[len(self.all)])
        copy.start()
        self.all.append(copy)
        return copy

    def wait(self):
        for copy in self.all:
            copy.wait()


class Plan:
    def __init__(self, seqs, members):
        assert members == 4 and seqs & (seqs - 1) == 0 and seqs >= 8
        self.seqs = seqs
        self.bits = seqs.bit_length() - 1
        self.stages = self.bits + 1
        self.blocks = 2 * seqs
        self.s = lax.axis_index("seq")
        self.member = lax.axis_index("qry")
        self.y, self.core = self.member // 2, self.member % 2
        self.info = jnp.stack([self.member, self.s, self.y, self.core]).astype(jnp.int32)

    def order(self, letters):
        return ["y" if letter == "y" else "xlh".index(letter) for letter in letters] + list(range(3, self.bits))

    def pairs(self, orders, step):
        out = []
        for s in range(self.seqs):
            for y in range(2):
                for core in range(2):
                    bit = self.order(orders[core])[step]
                    to = (s, y ^ 1) if bit == "y" else (s ^ (1 << bit), y)
                    out.append((s * 4 + y * 2 + core, to[0] * 4 + to[1] * 2 + core))
        return out

    def plain(self, grad, orders):
        rows, columns = grad.shape
        tail = (rows // self.seqs, columns // 4)
        parts = grad.reshape(self.seqs, tail[0], 2, 2, tail[1]).transpose(3, 0, 2, 1, 4)
        parts = parts.reshape((2,) + (2,) * self.stages + tail)
        own = {bit: (self.s >> bit) & 1 for bit in range(self.bits)} | {"y": self.y}
        axis = {bit: self.bits - bit for bit in range(self.bits)} | {"y": self.stages}
        for bit in own:
            parts = jnp.where(own[bit] == 1, jnp.flip(parts, axis[bit]), parts)
        both = [
            parts[core].transpose(*[axis[bit] - 1 for bit in self.order(orders[core])], self.stages, self.stages + 1)
            for core in range(2)
        ]
        parts = jnp.stack(both).reshape(2, self.blocks, *tail)
        kept = lax.dynamic_index_in_dim(parts, self.core, 0, keepdims=False)
        sent = lax.dynamic_index_in_dim(parts, 1 - self.core, 0, keepdims=False)
        return sent, kept


def place_of(order, info, s, y):
    place = 0
    for step, bit in enumerate(order):
        one = (info[2] ^ y) if bit == "y" else ((info[1] ^ s) >> bit) & 1
        place = place + (one << (len(order) - 1 - step))
    return place


class Scatter:
    def __init__(self, plan, orders, sent, kept):
        self.plan, self.orders, self.stage = plan, orders, 0
        self.terms = [kept, lax.ppermute(sent, "qry", [(q, q ^ 1) for q in range(4)])]

    def step(self, turn):
        plan = self.plan
        if self.stage == plan.stages:
            return
        self.terms = turn.wait(*self.terms)
        half = plan.blocks >> (self.stage + 1)
        leaving = functools.reduce(lambda a, b: a + b, [t[half : 2 * half] for t in self.terms])
        turn.done(leaving)
        self.terms = self.terms + [lax.ppermute(leaving, ("seq", "qry"), plan.pairs(self.orders, self.stage))]
        self.stage += 1

    def finish(self, turn):
        while self.stage < self.plan.stages:
            self.step(turn)
        self.terms = turn.wait(*self.terms)
        out = functools.reduce(lambda a, b: a + b, [t[0] for t in self.terms])
        turn.done(out)
        return out


class Turn:
    def __init__(self):
        self.last = []

    def wait(self, *values):
        if self.last:
            out = lax.optimization_barrier((*values, *self.last))
            values = out[: len(values)]
        return list(values)

    def done(self, *values):
        self.last = list(values)


def pick(ref, y, half):
    low = ref[:, y * 384 : y * 384 + 192]
    high = ref[:, y * 384 + 192 : y * 384 + 384]
    return jnp.where(half == 0, low, high)


def down_kernel(seqs, flip, orders, info, hidden, cot, out, turned, stage, sems):
    half = info[3] ^ flip
    for y in range(2):
        turned[y * 192 : (y + 1) * 192, :] = pick(cot, y, half).T
    width = FF // seqs
    copies = []
    for s in range(seqs):
        part = product(turned[...], hidden[:, s * width : (s + 1) * width])
        for y in range(2):
            place = jnp.where(half == 0, place_of(orders[0], info, s, y), place_of(orders[1], info, s, y))
            stage[s * 2 + y] = part[y * 192 : (y + 1) * 192]
            copy = pltpu.make_async_copy(stage.at[s * 2 + y], out.at[place], sems.at[s * 2 + y])
            copy.start()
            copies.append(copy)
    for copy in copies:
        copy.wait()


def in_kernel(seqs, flip, orders, info, normed, grad, out, turned, stage, sems):
    half = info[3] ^ flip
    turned[...] = normed[...].T
    height = D // seqs
    copies = []
    for y in range(2):
        start = pl.multiple_of((y * 2 + half) * D, 128)
        for n in range(3):
            part = product(turned[...], grad[:, pl.ds(pl.multiple_of(start + n * 256, 128), 256)])
            for s in range(seqs):
                stage[y * seqs + s, :, n * 256 : (n + 1) * 256] = part[s * height : (s + 1) * height]
        for s in range(seqs):
            place = jnp.where(half == 0, place_of(orders[0], info, s, y), place_of(orders[1], info, s, y))
            copy = pltpu.make_async_copy(stage.at[y * seqs + s], out.at[place], sems.at[y * seqs + s])
            copy.start()
            copies.append(copy)
    for copy in copies:
        copy.wait()


def square_kernel(seqs, flip, orders, info, normed_context, normed, mixed, gk, gv, gq, ga, out, turned_c, turned_a, turned_o, stage, sems):
    half = info[3] ^ flip
    turned_c[...] = normed_context[...].T
    turned_a[...] = normed[...].T
    turned_o[...] = mixed[...].T
    height = D // seqs
    copies = []
    for y in range(2):
        one = product(turned_c[...], jnp.concatenate([pick(gk, y, half), pick(gv, y, half)], axis=1))
        two = jnp.concatenate(
            [product(turned_a[...], pick(gq, y, half)), product(turned_o[...], pick(ga, y, half))], axis=1
        )
        for s in range(seqs):
            place = jnp.where(half == 0, place_of(orders[0], info, s, y), place_of(orders[1], info, s, y))
            stage[y * seqs + s, :height] = one[s * height : (s + 1) * height]
            stage[y * seqs + s, height:] = two[s * height : (s + 1) * height]
            copy = pltpu.make_async_copy(stage.at[y * seqs + s], out.at[place], sems.at[y * seqs + s])
            copy.start()
            copies.append(copy)
    for copy in copies:
        copy.wait()


def block_call(kernel, name, plan, flip, orders, args, rows, lanes, turned):
    orders = [plan.order(letters) for letters in orders]
    return pl.pallas_call(
        functools.partial(kernel, plan.seqs, flip, orders),
        out_shape=jax.ShapeDtypeStruct((plan.blocks, rows, lanes), F32),
        grid_spec=pltpu.PrefetchScalarGridSpec(
            num_scalar_prefetch=1,
            grid=(1,),
            in_specs=[vmem()] * len(args),
            out_specs=hbm(),
            scratch_shapes=[pltpu.VMEM(t, LOW) for t in turned]
            + [pltpu.VMEM((plan.blocks, rows, lanes), F32), pltpu.SemaphoreType.DMA((plan.blocks,))],
        ),
        compiler_params=pltpu.CompilerParams(vmem_limit_bytes=58 << 20),
        cost_estimate=SMALL,
        name=name,
    )(plan.info, *args)


def forward_kernel(
    info, context, query, context_seg, query_seg, gain_one, shift_one, b_query, b_value, b_out, gain_two, shift_two, b_in,
    w_query, w_key, w_value, w_out, w_in, context_cot, query_cot,
    o_cot, o_context, o_rows, o_query, o_key, o_value, o_weights, o_mixed, o_attended, o_normed, o_hidden, o_slope,
    v_wq, v_wk, v_wv, v_wo, v_win, sem_in,
    s_context, s_rows, s_query, s_key, s_value, s_weights, s_mixed, s_attended, s_normed, s_hidden, s_slope,
    turned_query, turned_value, turned_mixed, bias, diag, ahead, sem_out,
):
    count, fresh = context.shape[0], query.shape[0]
    total = s_rows.shape[0]
    own = total - fresh
    tiles = total // 128
    arrive = Copies(sem_in)
    loads = [
        arrive.start(source, target)
        for source, target in [(w_query, v_wq), (w_key, v_wk), (w_value, v_wv), (w_out, v_wo), (w_in, v_win)]
    ]
    leave = Copies(sem_out)
    send = leave.start
    send(context_cot.at[ds(info[0] * own, own), :], o_cot.at[:own, :])
    send(query_cot, o_cot.at[own:, :])
    gain, shift = wide(gain_one), wide(shift_one)

    def normalize(source, target, at, step):
        def one(i, carry):
            rows = pl.ds(pl.multiple_of(i * step, step), step)
            standard, _ = standardize(source[rows, :].astype(F32))
            target[pl.ds(pl.multiple_of(at + i * step, step), step), :] = (standard * gain + shift).astype(LOW)
            return carry
        lax.fori_loop(0, source.shape[0] // step, one, 0)

    normalize(context, s_context, 0, 64)
    normalize(query, s_rows, own, 64)
    s_rows[:own, :] = s_context[pl.ds(pl.multiple_of(info[0] * own, own), own), :]
    send(s_context, o_context)
    send(s_rows, o_rows)

    keys = jnp.broadcast_to(context_seg[...].astype(F32), (128, count)).T
    for t in range(tiles):
        if t * 128 < own:
            rows = context_seg[:, pl.ds(pl.multiple_of(info[0] * own + t * 128, 128), 128)]
        else:
            rows = query_seg[:, t * 128 - own : t * 128 - own + 128]
        bias[:, t * 128 : (t + 1) * 128] = jnp.where(keys == rows.astype(F32), 0.0, MASKED)

    loads[0].wait()
    for n in range(3):
        cols = slice(n * 256, (n + 1) * 256)
        part = product(s_rows[...], v_wq[:, cols]) + b_query[cols].astype(F32).reshape(1, -1)
        part = (part.astype(LOW) * jnp.asarray(SCALING, LOW))
        s_query[:, cols] = part
        turned_query[cols, :] = part.T
    send(s_query, o_query)
    loads[1].wait()
    for n in range(3):
        cols = slice(n * 256, (n + 1) * 256)
        s_key[:, cols] = product(s_context[...], v_wk[:, cols]).astype(LOW)
    send(s_key, o_key)
    loads[2].wait()
    for n in range(3):
        cols = slice(n * 256, (n + 1) * 256)
        part = (product(s_context[...], v_wv[:, cols]) + b_value[cols].astype(F32).reshape(1, -1)).astype(LOW)
        s_value[:, cols] = part
        turned_value[cols, :] = part.T
    send(s_value, o_value)

    diag[...] = jnp.zeros_like(diag)

    def attend(pair, carry):
        at = pl.ds(pl.multiple_of(pair * 128, 128), 128)
        key_pair = s_key[:, at]
        value_pair = turned_value[at, :]
        for t in range(tiles):
            cols = slice(t * 128, (t + 1) * 128)
            diag[:64, :128] = turned_query[pl.ds(pl.multiple_of(pair * 128, 64), 64), cols]
            diag[64:, 128:] = turned_query[pl.ds(pl.multiple_of(pair * 128 + 64, 64), 64), cols]
            scores = product(key_pair, diag[...])
            for half in range(2):
                lanes = slice(half * 128, (half + 1) * 128)
                part = scores[:, lanes] + bias[:, cols]
                raised = jnp.exp(part - jnp.max(part, axis=0, keepdims=True))
                scale = 1.0 / jnp.sum(raised, axis=0, keepdims=True)
                s_weights[pair, t, :, lanes] = (raised * scale).astype(LOW)
            both = product(value_pair, s_weights[pair, t])
            turned_mixed[pl.ds(pl.multiple_of(pair * 128, 64), 64), cols] = both[:64, :128].astype(LOW)
            turned_mixed[pl.ds(pl.multiple_of(pair * 128 + 64, 64), 64), cols] = both[64:, 128:].astype(LOW)
        return carry

    lax.fori_loop(0, PAIRS, attend, 0)
    send(s_weights, o_weights)
    for n in range(3):
        s_mixed[:, n * 256 : (n + 1) * 256] = turned_mixed[n * 256 : (n + 1) * 256, :].T
    send(s_mixed, o_mixed)
    loads[3].wait()
    for n in range(3):
        cols = slice(n * 256, (n + 1) * 256)
        s_attended[:, cols] = product(s_mixed[...], v_wo[:, cols]) + b_out[cols].astype(F32).reshape(1, -1)
    send(s_attended, o_attended)
    gain, shift = wide(gain_two), wide(shift_two)

    def second(i, carry):
        rows = pl.ds(pl.multiple_of(i * 64, 64), 64)

        def put(base):
            standard, _ = standardize(base.astype(F32) + s_attended[rows, :])
            s_normed[rows, :] = (standard * gain + shift).astype(LOW)

        @pl.when(i < own // 64)
        def _():
            put(context[pl.ds(pl.multiple_of(info[0] * own + i * 64, 64), 64), :])

        @pl.when(i >= own // 64)
        def _():
            put(query[pl.ds(pl.multiple_of(i * 64 - own, 64), 64), :])

        return carry

    lax.fori_loop(0, total // 64, second, 0)
    send(s_normed, o_normed)
    loads[4].wait()
    first = len(leave.all)
    steps = FF // 256

    def up(n, carry):
        cols = pl.ds(pl.multiple_of(n * 256, 256), 256)
        ahead[...] = product(s_normed[...], v_win[:, cols])
        for m in range(total // 64):
            rows = slice(m * 64, (m + 1) * 64)
            h = ahead[rows, :] + b_in[cols].astype(F32).reshape(1, -1)
            square = h * h
            t = jnp.tanh(h * (BEND + CUBE * square))
            half = 0.5 + 0.5 * t
            s_hidden[rows, cols] = (h * half).astype(LOW)
            bend = h * (BEND + 3 * CUBE * square)
            s_slope[rows, cols] = (half * (1.0 + bend * (1.0 - t))).astype(LOW)
        pltpu.make_async_copy(s_hidden.at[:, cols], o_hidden.at[:, cols], sem_out.at[first + 2 * n]).start()
        pltpu.make_async_copy(s_slope.at[:, cols], o_slope.at[:, cols], sem_out.at[first + 2 * n + 1]).start()
        return carry

    lax.fori_loop(0, steps, up, 0)

    def settle(n, carry):
        cols = pl.ds(pl.multiple_of(n * 256, 256), 256)
        pltpu.make_async_copy(s_hidden.at[:, cols], o_hidden.at[:, cols], sem_out.at[first + 2 * n]).wait()
        pltpu.make_async_copy(s_slope.at[:, cols], o_slope.at[:, cols], sem_out.at[first + 2 * n + 1]).wait()
        return carry

    lax.fori_loop(0, steps, settle, 0)
    leave.wait()

def forward(member, context, query, context_seg, query_seg, vectors, weights, cots):
    count, fresh = context.shape[0], query.shape[0]
    own = count // 4
    total = own + fresh
    kept = [
        ((count, D), LOW),
        ((total, D), LOW),
        ((total, D), LOW),
        ((count, D), LOW),
        ((count, D), LOW),
        ((PAIRS, total // 128, count, 256), LOW),
        ((total, D), LOW),
        ((total, D), F32),
        ((total, D), LOW),
        ((total, FF), LOW),
        ((total, FF), LOW),
    ]
    return pl.pallas_call(
        forward_kernel,
        out_shape=[jax.ShapeDtypeStruct((total, D), LOW)] + [jax.ShapeDtypeStruct(*s) for s in kept],
        grid_spec=pltpu.PrefetchScalarGridSpec(
            num_scalar_prefetch=1,
            grid=(1,),
            in_specs=[vmem()] * 12 + [hbm()] * 7,
            out_specs=[hbm()] * (len(kept) + 1),
            scratch_shapes=[pltpu.VMEM((D, D), LOW)] * 4
            + [pltpu.VMEM((D, FF), LOW), pltpu.SemaphoreType.DMA((5,))]
            + [pltpu.VMEM(*s) for s in kept]
            + [
                pltpu.VMEM((D, total), LOW),
                pltpu.VMEM((D, count), LOW),
                pltpu.VMEM((D, total), LOW),
                pltpu.VMEM((count, total), F32),
                pltpu.VMEM((128, 256), LOW),
                pltpu.VMEM((total, 256), F32),
                pltpu.SemaphoreType.DMA((11 + 2 * FF // 256,)),
            ],
        ),
        compiler_params=pltpu.CompilerParams(vmem_limit_bytes=58 << 20),
        cost_estimate=SMALL,
        name="forward",
    )(member, context, query, context_seg, query_seg, *vectors, *weights, *cots)


def hidden_kernel(cot, w_down, slope, out, sum_in, sum_down):
    for n in range(w_down.shape[0] // 256):
        cols = slice(n * 256, (n + 1) * 256)
        out[:, cols] = (transposed_right(cot[...], w_down[cols, :]) * slope[:, cols].astype(F32)).astype(LOW)
    sum_in[...] = whole(fold(out[...].astype(F32)))

    @pl.when(pl.program_id(0) == 0)
    def _():
        sum_down[...] = whole(fold(cot[...].astype(F32)))


def hidden_grad(cot, w_down, slope):
    total, step = cot.shape[0], 768
    return pl.pallas_call(
        hidden_kernel,
        out_shape=[
            jax.ShapeDtypeStruct((total, FF), LOW),
            jax.ShapeDtypeStruct((1, FF), F32),
            jax.ShapeDtypeStruct((1, D), F32),
        ],
        grid=(FF // step,),
        in_specs=[
            pl.BlockSpec((total, D), lambda i: (0, 0)),
            pl.BlockSpec((step, D), lambda i: (i, 0)),
            pl.BlockSpec((total, step), lambda i: (0, i)),
        ],
        out_specs=[
            pl.BlockSpec((total, step), lambda i: (0, i)),
            pl.BlockSpec((1, step), lambda i: (0, i)),
            pl.BlockSpec((1, D), lambda i: (0, 0)),
        ],
        compiler_params=pltpu.CompilerParams(vmem_limit_bytes=16 << 20),
        cost_estimate=SMALL,
        name="hidden_grad",
    )(cot, w_down, slope)


def branch_kernel(
    info, context, query, attended, cot, gain_two, grad_pre, w_in, w_out,
    o_after, o_branch, o_mixed, o_sums,
    v_win, v_wout, sem_in, normed,
):
    total, fresh = attended.shape[0], query.shape[0]
    own = total - fresh
    arrive = Copies(sem_in)
    loads = [arrive.start(w_in.at[n * 256 : (n + 1) * 256, :], v_win.at[n * 256 : (n + 1) * 256, :]) for n in range(3)]
    last = arrive.start(w_out, v_wout)
    for n in range(3):
        cols = slice(n * 256, (n + 1) * 256)
        loads[n].wait()
        normed[:, cols] = transposed_right(grad_pre[...], v_win[cols, :])
    gain = wide(gain_two)

    def back(i, carry, base):
        rows = ds(i * 32, 32)
        standard, inverse = standardize(base.astype(F32) + attended[rows, :])
        grad = normed[rows, :]
        after = cot[rows, :].astype(F32) + norm_pullback(standard, inverse, gain, grad)
        o_after[rows, :] = after
        low = after.astype(LOW)
        o_branch[rows, :] = low
        one, two, three = carry
        return one + fold(grad * standard), two + fold(grad), three + fold(low.astype(F32))

    zero = jnp.zeros((8, D), F32)
    sums = lax.fori_loop(
        0, own // 32, lambda i, c: back(i, c, context[ds(info[0] * own + i * 32, 32), :]), (zero, zero, zero)
    )
    sums = lax.fori_loop(own // 32, total // 32, lambda i, c: back(i, c, query[ds(i * 32 - own, 32), :]), sums)
    o_sums[...] = jnp.zeros_like(o_sums)
    o_sums[0:1, :], o_sums[1:2, :], o_sums[2:3, :] = whole(sums[2]), whole(sums[0]), whole(sums[1])
    last.wait()
    for n in range(3):
        cols = slice(n * 256, (n + 1) * 256)
        o_mixed[:, cols] = transposed_right(o_branch[...], v_wout[cols, :]).astype(LOW)


def branch_grad(member, context, query, attended, cot, gain_two, grad_pre, w_in, w_out):
    total = attended.shape[0]
    return pl.pallas_call(
        branch_kernel,
        out_shape=[
            jax.ShapeDtypeStruct((total, D), F32),
            jax.ShapeDtypeStruct((total, D), LOW),
            jax.ShapeDtypeStruct((total, D), LOW),
            jax.ShapeDtypeStruct((8, D), F32),
        ],
        grid_spec=pltpu.PrefetchScalarGridSpec(
            num_scalar_prefetch=1,
            grid=(1,),
            in_specs=[vmem()] * 6 + [hbm()] * 2,
            out_specs=[vmem()] * 4,
            scratch_shapes=[
                pltpu.VMEM((D, FF), LOW),
                pltpu.VMEM((D, D), LOW),
                pltpu.SemaphoreType.DMA((4,)),
                pltpu.VMEM((total, D), F32),
            ],
        ),
        compiler_params=pltpu.CompilerParams(vmem_limit_bytes=28 << 20),
        cost_estimate=SMALL,
        name="branch_grad",
    )(member, context, query, attended, cot, gain_two, grad_pre, w_in, w_out)


def attention_kernel(
    mixed, value, key, scaled_query, weights, o_query, o_key, o_value, o_sums,
    v_weights, sem_in, turned_mixed, turned_key, turned_query, scores, across, down_query, down_mixed,
):
    total = mixed.shape[0]
    tiles = total // 128
    arrive = Copies(sem_in)
    loads = [arrive.start(weights.at[pair], v_weights.at[pair]) for pair in range(PAIRS)]
    for n in range(3):
        cols = slice(n * 256, (n + 1) * 256)
        turned_mixed[cols, :] = mixed[:, cols].T
        turned_key[cols, :] = key[:, cols].T
    across[...] = jnp.zeros_like(across)
    lane = lax.broadcasted_iota(jnp.int32, (1, 128), 1)
    low_half = (lane < 64).astype(F32).astype(LOW)
    high_half = (lane >= 64).astype(F32).astype(LOW)
    for pair in range(PAIRS):
        at = slice(pair * 128, pair * 128 + 128)
        even, odd = slice(pair * 128, pair * 128 + 64), slice(pair * 128 + 64, pair * 128 + 128)
        value_pair, key_pair = value[:, at], turned_key[at, :]
        loads[pair].wait()
        for t in range(tiles):
            cols = slice(t * 128, (t + 1) * 128)
            across[t, :64, :128] = turned_mixed[even, cols]
            across[t, 64:, 128:] = turned_mixed[odd, cols]
            grad = product(value_pair, across[t])
            chance = v_weights[pair, t].astype(F32)
            both = chance * grad
            scores[t] = (both - chance * jnp.sum(both, axis=0, keepdims=True)).astype(LOW)
            part = product(key_pair, scores[t]) * SCALING
            turned_query[even, cols] = part[:64, :128].astype(LOW)
            turned_query[odd, cols] = part[64:, 128:].astype(LOW)
            for source, target in ((scaled_query, down_query), (mixed, down_mixed)):
                tile = source[cols, at]
                target[t * 256 : t * 256 + 128, :] = tile * low_half
                target[t * 256 + 128 : t * 256 + 256, :] = tile * high_half
        o_key[:, at] = sum(product(scores[t], down_query[t * 256 : (t + 1) * 256, :]) for t in range(tiles)).astype(LOW)
        o_value[:, at] = sum(
            product(v_weights[pair, t], down_mixed[t * 256 : (t + 1) * 256, :]) for t in range(tiles)
        ).astype(LOW)
    for n in range(3):
        o_query[:, n * 256 : (n + 1) * 256] = turned_query[n * 256 : (n + 1) * 256, :].T
    o_sums[...] = jnp.zeros_like(o_sums)
    o_sums[0:1, :] = whole(fold(o_query[...].astype(F32)))
    o_sums[1:2, :] = whole(fold(o_value[...].astype(F32)))


def attention_grad(mixed, value, key, scaled_query, weights):
    count, total = value.shape[0], mixed.shape[0]
    return pl.pallas_call(
        attention_kernel,
        out_shape=[
            jax.ShapeDtypeStruct((total, D), LOW),
            jax.ShapeDtypeStruct((count, D), LOW),
            jax.ShapeDtypeStruct((count, D), LOW),
            jax.ShapeDtypeStruct((8, D), F32),
        ],
        in_specs=[vmem()] * 4 + [hbm()],
        out_specs=[vmem()] * 4,
        scratch_shapes=[
            pltpu.VMEM(weights.shape, LOW),
            pltpu.SemaphoreType.DMA((PAIRS,)),
            pltpu.VMEM((D, total), LOW),
            pltpu.VMEM((D, count), LOW),
            pltpu.VMEM((D, total), LOW),
            pltpu.VMEM((total // 128, count, 256), LOW),
            pltpu.VMEM((total // 128, 128, 256), LOW),
            pltpu.VMEM((2 * total, 128), LOW),
            pltpu.VMEM((2 * total, 128), LOW),
        ],
        compiler_params=pltpu.CompilerParams(vmem_limit_bytes=28 << 20),
        cost_estimate=SMALL,
        name="attention_grad",
    )(mixed, value, key, scaled_query, weights)


def input_kernel(
    info, context, query, gain_one, after, grad_query, grad_key, grad_value, w_query, w_key, w_value,
    sums_one, sums_two, sum_in, sum_down, o_far, o_near, o_query, o_small, rows_grad, context_grad,
):
    count, fresh = context.shape[0], query.shape[0]
    own = count // 4
    for n in range(3):
        cols = slice(n * 256, (n + 1) * 256)
        rows_grad[:, cols] = transposed_right(grad_query[...], w_query[cols, :])
        context_grad[:, cols] = transposed_right(grad_key[...], w_key[cols, :]) + transposed_right(
            grad_value[...], w_value[cols, :]
        )
    gain = wide(gain_one)
    zero = jnp.zeros((8, D), F32)

    def pull(base, grad, carry):
        standard, inverse = standardize(base.astype(F32))
        one, two = carry
        return norm_pullback(standard, inverse, gain, grad), (one + fold(grad * standard), two + fold(grad))

    carry = (zero, zero)
    for r, target in enumerate((o_near.at[0], o_far.at[0], o_near.at[1], o_far.at[1])):

        def one(i, carry):
            rows = ds((info[0] ^ r) * own + i * 64, 64)
            grad = context_grad[rows, :]
            if r == 0:
                grad = grad + rows_grad[ds(i * 64, 64), :]
            out, carry = pull(context[rows, :], grad, carry)
            if r == 0:
                out = out + after[ds(i * 64, 64), :]
            target[ds(i * 64, 64), :] = out
            return carry

        carry = lax.fori_loop(0, own // 64, one, carry)

    def rest(i, carry):
        rows = ds(i * 64, 64)
        out, carry = pull(query[rows, :], rows_grad[ds(own + i * 64, 64), :], carry)
        o_query[rows, :] = out + after[ds(own + i * 64, 64), :]
        return carry

    carry = lax.fori_loop(0, fresh // 64, rest, carry)
    o_small[0:1, :], o_small[1:2, :] = whole(carry[0]), whole(carry[1])
    o_small[2:4, :] = sums_two[:2, :]
    o_small[4:7, :] = sums_one[:3, :]
    o_small[7:8, :] = sum_down[...]
    for j in range(4):
        o_small[8 + j : 9 + j, :] = sum_in[:, j * D : (j + 1) * D]
    o_small[12:, :] = jnp.zeros((4, D), F32)


def input_grad(member, args, own, fresh, count):
    shapes = [(2, own, D), (2, own, D), (fresh, D), (16, D)]
    return pl.pallas_call(
        input_kernel,
        out_shape=[jax.ShapeDtypeStruct(s, F32) for s in shapes],
        grid_spec=pltpu.PrefetchScalarGridSpec(
            num_scalar_prefetch=1,
            grid=(1,),
            in_specs=[vmem()] * len(args),
            out_specs=[vmem()] * 4,
            scratch_shapes=[pltpu.VMEM((own + fresh, D), F32), pltpu.VMEM((count, D), F32)],
        ),
        compiler_params=pltpu.CompilerParams(vmem_limit_bytes=24 << 20),
        cost_estimate=SMALL,
        name="input_grad",
    )(member, *args)


def body(
    context_in,
    query_in,
    context_seg,
    query_seg,
    attn_gain,
    attn_shift,
    w_query,
    b_query,
    w_key,
    w_value,
    b_value,
    w_out,
    b_out,
    mlp_gain,
    mlp_shift,
    w_in,
    b_in,
    w_down,
    b_down,
    context_cot,
    query_cot,
):
    count, fresh = context_in.shape[1], query_in.shape[1]
    seqs = lax.axis_size("seq")
    plan = Plan(seqs, lax.axis_size("qry"))
    own = count // 4
    total = own + fresh
    index, member = plan.member, plan.info
    context, query = context_in[0], query_in[0]
    direct = FF // seqs % 128 == 0
    turn = Turn()

    cot, context_low, rows_low, scaled_query, keys, values, weights, mixed, attended, normed_two, hidden, slope = forward(
        member,
        context,
        query,
        context_seg,
        query_seg,
        (attn_gain, attn_shift, b_query, b_value, b_out, mlp_gain, mlp_shift, b_in),
        (w_query, w_key, w_value, w_out, w_in),
        (context_cot[0], query_cot[0]),
    )
    turn.done(hidden)

    orders = {"down": ("lhxy", "xlyh"), "in": ("xhyl", "yhxl"), "square": ("xlyh", "yxlh")}

    def half(flip, kernel, name, args, rows, lanes, turned):
        out = block_call(kernel, name + "_grad", plan, flip, orders[name], turn.wait(*args), rows, lanes, turned)
        turn.done(out)
        return out

    def scatter(name, *parts):
        return [Scatter(plan, orders[name], *part) for part in parts]

    def spread(name, *products):
        return scatter(name, *[plan.plain(transposed_left(*one), orders[name]) for one in products])

    def step(group):
        for one in group:
            one.step(turn)

    down_call = (down_kernel, "down", (hidden, cot), 192, FF // seqs, [(384, total)])
    if direct:
        down_sent = half(1, *down_call)
    cot_now, slope_now = turn.wait(cot, slope)
    grad_pre, sum_in, sum_down = hidden_grad(cot_now, w_down, slope_now)
    turn.done(grad_pre)
    in_call = (in_kernel, "in", (normed_two, grad_pre), D // seqs, D, [(D, total)])
    if direct:
        in_sent = half(1, *in_call)
        downs = scatter("down", (down_sent, half(0, *down_call)))
    else:
        downs = spread("down", (hidden, cot))
    step(downs)
    if direct:
        ins = scatter("in", (in_sent, half(0, *in_call)))
    else:
        ins = spread("in", (normed_two, grad_pre))
    (grad_pre_now,) = turn.wait(grad_pre)
    grad_after, branch, grad_mixed, sums_one = branch_grad(
        member, context, query, attended, cot, mlp_gain, grad_pre_now, w_in, w_out
    )
    turn.done(grad_mixed)
    step(ins)
    (grad_mixed_now,) = turn.wait(grad_mixed)
    grad_query, grad_keys, grad_values, sums_two = attention_grad(
        grad_mixed_now, values, keys, scaled_query, weights
    )
    turn.done(grad_query)
    step(downs)
    square_call = (
        square_kernel,
        "square",
        (context_low, rows_low, mixed, grad_keys, grad_values, grad_query, branch),
        2 * D // seqs,
        384,
        [(D, count), (D, total), (D, total)],
    )
    if direct:
        square_sent = half(1, *square_call)
        squares = scatter("square", (square_sent, half(0, *square_call)))
    else:
        squares = spread(
            "square", (context_low, grad_keys), (context_low, grad_values), (rows_low, grad_query), (mixed, branch)
        )
    (grad_query_now,) = turn.wait(grad_query)
    far, near, query_grad, small = input_grad(
        member,
        (
            context, query, attn_gain, grad_after, grad_query_now, grad_keys, grad_values,
            w_query, w_key, w_value, sums_one, sums_two, sum_in, sum_down,
        ),
        own,
        fresh,
        count,
    )
    turn.done(query_grad)
    core_pairs = [(q, q ^ 1) for q in range(4)]
    y_pairs = [(q, q ^ 2) for q in range(4)]
    received = lax.ppermute(far, "qry", core_pairs)
    small_far = lax.ppermute(small, "qry", core_pairs)

    def small_step(stage):
        nonlocal small, small_far
        small, small_far = turn.wait(small, small_far)
        small = small + small_far
        turn.done(small)
        if stage < plan.stages:
            small_far = lax.ppermute(small, ("seq", "qry"), plan.pairs(orders["square"], stage))

    step(squares)
    near, received = turn.wait(near, received)
    pair = near + received
    turn.done(pair)
    pair_far = lax.ppermute(pair, "qry", y_pairs)
    small_step(0)
    step(downs)
    (hidden_now,) = turn.wait(hidden)
    added = attended + product(hidden_now, w_down) + b_down.astype(F32)
    turn.done(added)
    out_far = lax.ppermute(added[:own], "qry", y_pairs)
    step(ins)
    step(downs)
    pair, pair_far = turn.wait(pair, pair_far)
    grad_pair = pair + pair_far[::-1]
    turn.done(grad_pair)
    grad_near = lax.ppermute(grad_pair, "qry", core_pairs)
    step(ins)
    step(squares)
    small_step(1)
    added_own, out_far = turn.wait(added[:own], out_far)
    out_pair = jnp.stack([added_own, out_far])
    turn.done(out_pair)
    out_near = lax.ppermute(out_pair, "qry", core_pairs)
    step(ins)
    step(squares)
    small_step(2)
    grad_down = downs[0].finish(turn)
    if direct:
        grad_down = grad_down.T
    step(squares)
    small_step(3)
    grad_in = ins[0].finish(turn)
    for stage in range(4, plan.stages + 1):
        small_step(stage)
    square = [one.finish(turn) for one in squares]
    if direct:
        height = D // seqs
        grad_w_key, grad_w_value = square[0][:height, :192], square[0][:height, 192:]
        grad_w_query, grad_w_out = square[0][height:, :192], square[0][height:, 192:]
    else:
        grad_w_key, grad_w_value, grad_w_query, grad_w_out = square

    def place(pair, near):
        parts = jnp.stack([pair[0], near[0], pair[1], near[1]])
        return jnp.concatenate([lax.dynamic_index_in_dim(parts, index ^ j, 0, keepdims=False) for j in range(4)], axis=0)

    context_grad = place(grad_pair, grad_near)
    context_out = (context.astype(F32) + place(out_pair, out_near)).astype(LOW)
    query_out = (query.astype(F32) + added[own:]).astype(LOW)
    return (
        context_out[None],
        query_out[None],
        context_grad[None],
        query_grad[None],
        small[0],
        small[1],
        grad_w_query,
        small[2],
        grad_w_key,
        grad_w_value,
        small[3],
        grad_w_out,
        small[4],
        small[5],
        small[6],
        grad_in,
        small[8:12].reshape(-1),
        grad_down,
        small[7],
    )


def solution(mesh):
    placed = (
        P("seq", None, None),
        P("seq", "qry", None),
        P("seq", None),
        P("seq", "qry"),
        P(),
        P(),
        P(),
        P(),
        P(),
        P(),
        P(),
        P(),
        P(),
        P(),
        P(),
        P(),
        P(),
        P(),
        P(),
        P("seq", None, None),
        P("seq", "qry", None),
    )
    return jax.shard_map(
        body,
        mesh=mesh,
        in_specs=placed,
        out_specs=(
            P("seq", None, None),
            P("seq", "qry", None),
            P("seq", None, None),
            P("seq", "qry", None),
            P(),
            P(),
            P("seq", "qry"),
            P(),
            P("seq", "qry"),
            P("seq", "qry"),
            P(),
            P("seq", "qry"),
            P(),
            P(),
            P(),
            P("seq", "qry"),
            P(),
            P("seq", "qry"),
            P(),
        ),
        check_vma=False,
    )
```

```python
import functools

import jax
import jax.numpy as jnp
from jax import lax
from jax.experimental import pallas as pl
from jax.experimental.pallas import tpu as pltpu
from jax.sharding import PartitionSpec as P

D = 768
HEADS = 12
HEAD_DIM = 64
FF = 3072
PAIRS = HEADS // 2

EPSILON = 1e-05
MASKED = -1e30
LOW = jnp.bfloat16
F32 = jnp.float32
SCALING = HEAD_DIM ** (-0.5)
BEND = 0.7978845608028654
CUBE = 0.044715 * BEND


def standardize(values):
    center = values - jnp.mean(values, axis=-1, keepdims=True)
    spread = jnp.mean(center * center, axis=-1, keepdims=True)
    inverse = lax.rsqrt(spread + EPSILON)
    return center * inverse, inverse


def norm_pullback(standard, inverse, gain, grad):
    scaled = grad * gain
    first = jnp.mean(scaled, axis=-1, keepdims=True)
    second = jnp.mean(scaled * standard, axis=-1, keepdims=True)
    return inverse * (scaled - first - standard * second)


def product(left, right):
    return jnp.dot(left, right, preferred_element_type=F32)


def transposed_left(left, right):
    return lax.dot_general(left, right, (((0,), (0,)), ((), ())), preferred_element_type=F32)


def transposed_right(left, right):
    return lax.dot_general(left, right, (((1,), (1,)), ((), ())), preferred_element_type=F32)


def wide(ref):
    return ref[...].astype(F32).reshape(1, -1)


def ds(start, size):
    return pl.ds(pl.multiple_of(start, size), size)


def fold(values):
    return jnp.sum(values.reshape(values.shape[0] // 8, 8, values.shape[1]), axis=0)


def whole(values):
    return jnp.sum(values, axis=0, keepdims=True)


def vmem():
    return pl.BlockSpec(memory_space=pltpu.VMEM)


def hbm():
    return pl.BlockSpec(memory_space=pltpu.HBM)


SMALL = pl.CostEstimate(flops=0, bytes_accessed=0, transcendentals=0)


LIMIT = 28


class Copies:
    def __init__(self, sems):
        self.sems, self.all = sems, []

    def start(self, source, target):
        copy = pltpu.make_async_copy(source, target, self.sems.at[len(self.all)])
        copy.start()
        self.all.append(copy)
        return copy

    def wait(self):
        for copy in self.all:
            copy.wait()


class Plan:
    def __init__(self, seqs, members):
        assert members == 4 and seqs & (seqs - 1) == 0 and seqs >= 8
        self.seqs = seqs
        self.bits = seqs.bit_length() - 1
        self.stages = self.bits + 1
        self.blocks = 2 * seqs
        self.s = lax.axis_index("seq")
        self.member = lax.axis_index("qry")
        self.y, self.core = self.member // 2, self.member % 2
        self.info = jnp.stack([self.member, self.s, self.y, self.core]).astype(jnp.int32)

    def order(self, letters):
        return ["y" if letter == "y" else "xlh".index(letter) for letter in letters] + list(range(3, self.bits))

    def pairs(self, orders, step):
        out = []
        for s in range(self.seqs):
            for y in range(2):
                for core in range(2):
                    bit = self.order(orders[core])[step]
                    to = (s, y ^ 1) if bit == "y" else (s ^ (1 << bit), y)
                    out.append((s * 4 + y * 2 + core, to[0] * 4 + to[1] * 2 + core))
        return out

    def plain(self, grad, orders):
        rows, columns = grad.shape
        tail = (rows // self.seqs, columns // 4)
        parts = grad.reshape(self.seqs, tail[0], 2, 2, tail[1]).transpose(3, 0, 2, 1, 4)
        parts = parts.reshape((2,) + (2,) * self.stages + tail)
        own = {bit: (self.s >> bit) & 1 for bit in range(self.bits)} | {"y": self.y}
        axis = {bit: self.bits - bit for bit in range(self.bits)} | {"y": self.stages}
        for bit in own:
            parts = jnp.where(own[bit] == 1, jnp.flip(parts, axis[bit]), parts)
        both = [
            parts[core].transpose(*[axis[bit] - 1 for bit in self.order(orders[core])], self.stages, self.stages + 1)
            for core in range(2)
        ]
        parts = jnp.stack(both).reshape(2, self.blocks, *tail)
        kept = lax.dynamic_index_in_dim(parts, self.core, 0, keepdims=False)
        sent = lax.dynamic_index_in_dim(parts, 1 - self.core, 0, keepdims=False)
        return [sent], kept


def place_of(order, info, s, y):
    place = 0
    for step, bit in enumerate(order):
        one = (info[2] ^ y) if bit == "y" else ((info[1] ^ s) >> bit) & 1
        place = place + (one << (len(order) - 1 - step))
    return place


class Scatter:
    def __init__(self, plan, orders, sent, kept):
        self.plan, self.orders, self.stage = plan, orders, 0
        pairs = [(q, q ^ 1) for q in range(4)]
        self.terms = [kept] + [lax.ppermute(piece, "qry", pairs) for piece in sent]
        self.pieces = len(sent)

    def step(self, turn):
        plan = self.plan
        if self.stage == plan.stages:
            return
        self.terms = turn.wait(*self.terms)
        half = plan.blocks >> (self.stage + 1)
        leaving = self.sum(half, 2 * half)
        turn.done(leaving)
        self.terms = self.terms + [lax.ppermute(leaving, ("seq", "qry"), plan.pairs(self.orders, self.stage))]
        self.stage += 1

    def sum(self, low, high):
        size = self.plan.blocks // self.pieces
        span = [self.terms[1 + i] for i in range(low // size, -(-high // size))]
        near = span[0][low % size : low % size + high - low] if len(span) == 1 else jnp.concatenate(span, axis=0)
        return functools.reduce(lambda a, b: a + b, [t[low:high] for t in self.terms[1 + self.pieces :]], self.terms[0][low:high] + near)

    def finish(self, turn):
        while self.stage < self.plan.stages:
            self.step(turn)
        self.terms = turn.wait(*self.terms)
        out = self.sum(0, 1)[0]
        turn.done(out)
        return out


class Turn:
    def __init__(self):
        self.last = []

    def wait(self, *values):
        if self.last:
            out = lax.optimization_barrier((*values, *self.last))
            values = out[: len(values)]
        return list(values)

    def done(self, *values):
        self.last = list(values)


def pick(ref, y, half):
    low = ref[:, y * 384 : y * 384 + 192]
    high = ref[:, y * 384 + 192 : y * 384 + 384]
    return jnp.where(half == 0, low, high)


def down_kernel(setup, info, hidden, cot, *rest):
    seqs, outs, (turned, stage, sems) = setup.seqs, rest[: setup.outs], rest[setup.outs :]
    width = FF // seqs
    leaves = []
    for side, half in setup.halves(info):
        leave = Blocks(setup, side, outs, sems)
        for y in range(2):
            turned[y * 192 : (y + 1) * 192, :] = pick(cot, y, half).T
        for s in range(seqs):
            part = product(turned[...], hidden[:, s * width : (s + 1) * width])
            for y in range(2):
                at = leave.at(s, y)
                stage[at] = part[y * 192 : (y + 1) * 192]
                leave.start(stage, at, setup.place(half, info, s, y))
        leaves.append(leave)
    for leave in leaves:
        leave.wait(stage)


def in_kernel(setup, info, normed, grad, *rest):
    seqs, outs, (turned, stage, sems) = setup.seqs, rest[: setup.outs], rest[setup.outs :]
    turned[...] = normed[...].T
    height = D // seqs
    leaves = []
    for side, half in setup.halves(info):
        leave = Blocks(setup, side, outs, sems)
        for y in range(2):
            start = pl.multiple_of((y * 2 + half) * D, 128)
            for n in range(3):
                part = product(turned[...], grad[:, pl.ds(pl.multiple_of(start + n * 256, 128), 256)])
                for s in range(seqs):
                    stage[leave.at(s, y), :, n * 256 : (n + 1) * 256] = part[s * height : (s + 1) * height]
            for s in range(seqs):
                leave.start(stage, leave.at(s, y), setup.place(half, info, s, y))
        leaves.append(leave)
    for leave in leaves:
        leave.wait(stage)


def square_kernel(setup, info, normed_context, normed, mixed, gk, gv, gq, ga, *rest):
    seqs, outs, (turned_c, turned_a, turned_o, stage, sems) = setup.seqs, rest[: setup.outs], rest[setup.outs :]
    turned_c[...] = normed_context[...].T
    turned_a[...] = normed[...].T
    turned_o[...] = mixed[...].T
    height = D // seqs
    leaves = []
    for side, half in setup.halves(info):
        leave = Blocks(setup, side, outs, sems)
        for y in range(2):
            one = product(turned_c[...], jnp.concatenate([pick(gk, y, half), pick(gv, y, half)], axis=1))
            for s in range(seqs):
                stage[leave.at(s, y), :height] = one[s * height : (s + 1) * height]
            two = jnp.concatenate(
                [product(turned_a[...], pick(gq, y, half)), product(turned_o[...], pick(ga, y, half))], axis=1
            )
            for s in range(seqs):
                stage[leave.at(s, y), height:] = two[s * height : (s + 1) * height]
                leave.start(stage, leave.at(s, y), setup.place(half, info, s, y))
        leaves.append(leave)
    for leave in leaves:
        leave.wait(stage)


class Setup:
    def __init__(self, plan, orders, sides, pieces):
        self.seqs, self.sides, self.pieces = plan.seqs, sides, pieces
        self.orders = [plan.order(letters) for letters in orders]
        self.blocks = plan.blocks
        self.counts = [pieces if side else 1 for side in sides]
        self.outs = sum(self.counts)

    def halves(self, info):
        return [(i, info[3] ^ side) for i, side in enumerate(self.sides)]

    def place(self, half, info, s, y):
        one, two = [place_of(order, info, s, y) for order in self.orders]
        return jnp.where(half == 0, one, two)


class Blocks:
    def __init__(self, setup, side, outs, sems):
        before = sum(setup.counts[:side])
        self.outs, self.sems, self.all = outs[before : before + setup.counts[side]], sems, []
        self.first, self.seqs = side * setup.blocks, setup.seqs

    def at(self, s, y):
        return self.first + s * 2 + y

    def each(self, stage, at, place, act):
        size = self.outs[0].shape[0]
        if len(self.outs) == 1:
            act(pltpu.make_async_copy(stage.at[at], self.outs[0].at[place], self.sems.at[at]))
            return
        for i, out in enumerate(self.outs):

            @pl.when((place >= i * size) & (place < (i + 1) * size))
            def _():
                act(pltpu.make_async_copy(stage.at[at], out.at[place - i * size], self.sems.at[at]))

    def start(self, stage, at, place):
        self.all.append((at, place))
        self.each(stage, at, place, lambda copy: copy.start())

    def wait(self, stage):
        for at, place in self.all:
            self.each(stage, at, place, lambda copy: copy.wait())


def block_call(kernel, name, plan, setup, args, rows, lanes, turned):
    blocks = plan.blocks * len(setup.sides)
    shapes = []
    for count in setup.counts:
        shapes += [pltpu.HBM((plan.blocks // count, rows, lanes), F32)] * count
    return pl.pallas_call(
        functools.partial(kernel, setup),
        out_shape=shapes,
        grid_spec=pltpu.PrefetchScalarGridSpec(
            num_scalar_prefetch=1,
            grid=(1,),
            in_specs=[vmem()] * len(args),
            out_specs=[hbm()] * len(shapes),
            scratch_shapes=[pltpu.VMEM(t, LOW) for t in turned]
            + [pltpu.VMEM((blocks, rows, lanes), F32), pltpu.SemaphoreType.DMA((blocks,))],
        ),
        compiler_params=pltpu.CompilerParams(vmem_limit_bytes=LIMIT << 20),
        cost_estimate=SMALL,
        name=name,
    )(plan.info, *args)


def forward_kernel(
    info, context, query, context_seg, query_seg, gain_one, shift_one, b_query, b_value, b_out, gain_two, shift_two, b_in,
    w_query, w_key, w_value, w_out, w_in, context_cot, query_cot,
    o_cot, o_context, o_rows, o_query, o_key, o_value, o_weights, o_mixed, o_attended, o_normed, o_hidden, o_slope,
    v_wq, v_wk, v_wv, v_wo, v_win, sem_in,
    s_cot, s_context, s_rows, s_query, s_key, s_value, s_weights, s_mixed, s_attended, s_normed, s_hidden, s_slope,
    turned_query, turned_value, turned_mixed, bias, diag, scores, ahead, sem_out,
):
    count, fresh = context.shape[0], query.shape[0]
    total = s_rows.shape[0]
    own = total - fresh
    tiles = total // 128
    arrive = Copies(sem_in)
    loads = [
        arrive.start(source, target)
        for source, target in [
            (w_query, v_wq),
            (w_key, v_wk),
            (w_value, v_wv),
            (w_out, v_wo),
            (w_in, v_win),
            (context_cot.at[ds(info[0] * own, own), :], s_cot.at[:own, :]),
            (query_cot, s_cot.at[own:, :]),
        ]
    ]
    leave = Copies(sem_out)
    send = leave.start
    gain, shift = wide(gain_one), wide(shift_one)

    def normalize(source, target, at, step):
        def one(i, carry):
            rows = pl.ds(pl.multiple_of(i * step, step), step)
            standard, _ = standardize(source[rows, :].astype(F32))
            target[pl.ds(pl.multiple_of(at + i * step, step), step), :] = (standard * gain + shift).astype(LOW)
            return carry
        lax.fori_loop(0, source.shape[0] // step, one, 0)

    normalize(context, s_context, 0, 64)
    normalize(query, s_rows, own, 64)
    s_rows[:own, :] = s_context[pl.ds(pl.multiple_of(info[0] * own, own), own), :]
    send(s_context, o_context)
    send(s_rows, o_rows)

    keys = jnp.broadcast_to(context_seg[...].astype(F32), (128, count)).T
    for t in range(tiles):
        if t * 128 < own:
            rows = context_seg[:, pl.ds(pl.multiple_of(info[0] * own + t * 128, 128), 128)]
        else:
            rows = query_seg[:, t * 128 - own : t * 128 - own + 128]
        bias[:, t * 128 : (t + 1) * 128] = jnp.where(keys == rows.astype(F32), 0.0, MASKED)

    loads[0].wait()
    for n in range(3):
        cols = slice(n * 256, (n + 1) * 256)
        part = product(s_rows[...], v_wq[:, cols]) + b_query[cols].astype(F32).reshape(1, -1)
        part = (part.astype(LOW) * jnp.asarray(SCALING, LOW))
        s_query[:, cols] = part
        turned_query[cols, :] = part.T
    send(s_query, o_query)
    loads[1].wait()
    for n in range(3):
        cols = slice(n * 256, (n + 1) * 256)
        s_key[:, cols] = product(s_context[...], v_wk[:, cols]).astype(LOW)
    send(s_key, o_key)
    loads[2].wait()
    for n in range(3):
        cols = slice(n * 256, (n + 1) * 256)
        part = (product(s_context[...], v_wv[:, cols]) + b_value[cols].astype(F32).reshape(1, -1)).astype(LOW)
        s_value[:, cols] = part
        turned_value[cols, :] = part.T
    send(s_value, o_value)
    loads[5].wait()
    loads[6].wait()
    send(s_cot, o_cot)

    diag[...] = jnp.zeros_like(diag)

    steps = [(pair, t) for pair in range(PAIRS) for t in range(tiles)]

    def parts(pair):
        return slice(pair * 128, pair * 128 + 64), slice(pair * 128 + 64, pair * 128 + 128)

    def score(i):
        (pair, t), (even, odd) = steps[i], parts(steps[i][0])
        diag[i % 2, :64, :128] = turned_query[even, t * 128 : (t + 1) * 128]
        diag[i % 2, 64:, 128:] = turned_query[odd, t * 128 : (t + 1) * 128]
        scores[i % 2] = product(s_key[:, pair * 128 : pair * 128 + 128], diag[i % 2])

    def weigh(i):
        pair, t = steps[i]
        for side in range(2):
            lanes = slice(side * 128, (side + 1) * 128)
            part = scores[i % 2, :, lanes] + bias[:, t * 128 : (t + 1) * 128]
            raised = jnp.exp(part - jnp.max(part, axis=0, keepdims=True))
            scale = 1.0 / jnp.sum(raised, axis=0, keepdims=True)
            s_weights[pair, t, :, lanes] = (raised * scale).astype(LOW)

    def mix(i):
        (pair, t), (even, odd) = steps[i], parts(steps[i][0])
        both = product(turned_value[pair * 128 : pair * 128 + 128, :], s_weights[pair, t])
        turned_mixed[even, t * 128 : (t + 1) * 128] = both[:64, :128].astype(LOW)
        turned_mixed[odd, t * 128 : (t + 1) * 128] = both[64:, 128:].astype(LOW)
        if t == tiles - 1:
            send(s_weights.at[pair], o_weights.at[pair])

    score(0)
    for i in range(len(steps)):
        if i + 1 < len(steps):
            score(i + 1)
        weigh(i)
        if i > 0:
            mix(i - 1)
    mix(len(steps) - 1)
    for n in range(3):
        s_mixed[:, n * 256 : (n + 1) * 256] = turned_mixed[n * 256 : (n + 1) * 256, :].T
    send(s_mixed, o_mixed)
    loads[3].wait()
    for n in range(3):
        cols = slice(n * 256, (n + 1) * 256)
        s_attended[:, cols] = product(s_mixed[...], v_wo[:, cols]) + b_out[cols].astype(F32).reshape(1, -1)
    send(s_attended, o_attended)
    gain, shift = wide(gain_two), wide(shift_two)

    def second(i, carry):
        rows = pl.ds(pl.multiple_of(i * 64, 64), 64)

        def put(base):
            standard, _ = standardize(base.astype(F32) + s_attended[rows, :])
            s_normed[rows, :] = (standard * gain + shift).astype(LOW)

        @pl.when(i < own // 64)
        def _():
            put(context[pl.ds(pl.multiple_of(info[0] * own + i * 64, 64), 64), :])

        @pl.when(i >= own // 64)
        def _():
            put(query[pl.ds(pl.multiple_of(i * 64 - own, 64), 64), :])

        return carry

    lax.fori_loop(0, total // 64, second, 0)
    send(s_normed, o_normed)
    loads[4].wait()
    steps = FF // 256
    ahead[0] = product(s_normed[...], v_win[:, :256])
    for n in range(steps):
        cols = slice(n * 256, (n + 1) * 256)
        if n + 1 < steps:
            ahead[(n + 1) % 2] = product(s_normed[...], v_win[:, (n + 1) * 256 : (n + 2) * 256])
        extra = b_in[cols].astype(F32).reshape(1, -1)
        for m in range(total // 64):
            rows = slice(m * 64, (m + 1) * 64)
            h = ahead[n % 2, rows, :] + extra
            square = h * h
            t = jnp.tanh(h * (BEND + CUBE * square))
            part = 0.5 + 0.5 * t
            s_hidden[rows, cols] = (h * part).astype(LOW)
            bend = h * (BEND + 3 * CUBE * square)
            s_slope[rows, cols] = (part * (1.0 + bend * (1.0 - t))).astype(LOW)
        send(s_hidden.at[:, cols], o_hidden.at[:, cols])
        send(s_slope.at[:, cols], o_slope.at[:, cols])
    leave.wait()

def forward(member, context, query, context_seg, query_seg, vectors, weights, cots):
    count, fresh = context.shape[0], query.shape[0]
    own = count // 4
    total = own + fresh
    kept = [
        ((total, D), LOW),
        ((count, D), LOW),
        ((total, D), LOW),
        ((total, D), LOW),
        ((count, D), LOW),
        ((count, D), LOW),
        ((PAIRS, total // 128, count, 256), LOW),
        ((total, D), LOW),
        ((total, D), F32),
        ((total, D), LOW),
        ((total, FF), LOW),
        ((total, FF), LOW),
    ]
    return pl.pallas_call(
        forward_kernel,
        out_shape=[jax.ShapeDtypeStruct(*s) for s in kept],
        grid_spec=pltpu.PrefetchScalarGridSpec(
            num_scalar_prefetch=1,
            grid=(1,),
            in_specs=[vmem()] * 12 + [hbm()] * 7,
            out_specs=[hbm()] * len(kept),
            scratch_shapes=[pltpu.VMEM((D, D), LOW)] * 4
            + [pltpu.VMEM((D, FF), LOW), pltpu.SemaphoreType.DMA((7,))]
            + [pltpu.VMEM(*s) for s in kept]
            + [
                pltpu.VMEM((D, total), LOW),
                pltpu.VMEM((D, count), LOW),
                pltpu.VMEM((D, total), LOW),
                pltpu.VMEM((count, total), F32),
                pltpu.VMEM((2, 128, 256), LOW),
                pltpu.VMEM((2, count, 256), F32),
                pltpu.VMEM((2, total, 256), F32),
                pltpu.SemaphoreType.DMA((9 + PAIRS + 2 * FF // 256,)),
            ],
        ),
        compiler_params=pltpu.CompilerParams(vmem_limit_bytes=58 << 20),
        cost_estimate=SMALL,
        name="forward",
    )(member, context, query, context_seg, query_seg, *vectors, *weights, *cots)


def hidden_kernel(cot, w_down, slope, out, sum_in, sum_down):
    for n in range(w_down.shape[0] // 256):
        cols = slice(n * 256, (n + 1) * 256)
        out[:, cols] = (transposed_right(cot[...], w_down[cols, :]) * slope[:, cols].astype(F32)).astype(LOW)
    sum_in[...] = whole(fold(out[...].astype(F32)))

    @pl.when(pl.program_id(0) == 0)
    def _():
        sum_down[...] = whole(fold(cot[...].astype(F32)))


def hidden_grad(cot, w_down, slope):
    total, step = cot.shape[0], 768
    return pl.pallas_call(
        hidden_kernel,
        out_shape=[
            jax.ShapeDtypeStruct((total, FF), LOW),
            jax.ShapeDtypeStruct((1, FF), F32),
            jax.ShapeDtypeStruct((1, D), F32),
        ],
        grid=(FF // step,),
        in_specs=[
            pl.BlockSpec((total, D), lambda i: (0, 0)),
            pl.BlockSpec((step, D), lambda i: (i, 0)),
            pl.BlockSpec((total, step), lambda i: (0, i)),
        ],
        out_specs=[
            pl.BlockSpec((total, step), lambda i: (0, i)),
            pl.BlockSpec((1, step), lambda i: (0, i)),
            pl.BlockSpec((1, D), lambda i: (0, 0)),
        ],
        compiler_params=pltpu.CompilerParams(vmem_limit_bytes=16 << 20),
        cost_estimate=SMALL,
        name="hidden_grad",
    )(cot, w_down, slope)


def branch_kernel(
    info, context, query, attended, cot, gain_two, grad_pre, w_in, w_out,
    o_after, o_branch, o_mixed, o_sums,
    v_win, v_wout, sem_in, normed,
):
    total, fresh = attended.shape[0], query.shape[0]
    own = total - fresh
    arrive = Copies(sem_in)
    loads = [arrive.start(w_in.at[n * 256 : (n + 1) * 256, :], v_win.at[n * 256 : (n + 1) * 256, :]) for n in range(3)]
    last = arrive.start(w_out, v_wout)
    for n in range(3):
        cols = slice(n * 256, (n + 1) * 256)
        loads[n].wait()
        normed[:, cols] = transposed_right(grad_pre[...], v_win[cols, :])
    gain = wide(gain_two)

    def back(i, carry, base):
        rows = ds(i * 32, 32)
        standard, inverse = standardize(base.astype(F32) + attended[rows, :])
        grad = normed[rows, :]
        after = cot[rows, :].astype(F32) + norm_pullback(standard, inverse, gain, grad)
        o_after[rows, :] = after
        low = after.astype(LOW)
        o_branch[rows, :] = low
        one, two, three = carry
        return one + fold(grad * standard), two + fold(grad), three + fold(low.astype(F32))

    zero = jnp.zeros((8, D), F32)
    sums = lax.fori_loop(
        0, own // 32, lambda i, c: back(i, c, context[ds(info[0] * own + i * 32, 32), :]), (zero, zero, zero)
    )
    sums = lax.fori_loop(own // 32, total // 32, lambda i, c: back(i, c, query[ds(i * 32 - own, 32), :]), sums)
    o_sums[...] = jnp.zeros_like(o_sums)
    o_sums[0:1, :], o_sums[1:2, :], o_sums[2:3, :] = whole(sums[2]), whole(sums[0]), whole(sums[1])
    last.wait()
    for n in range(3):
        cols = slice(n * 256, (n + 1) * 256)
        o_mixed[:, cols] = transposed_right(o_branch[...], v_wout[cols, :]).astype(LOW)


def branch_grad(member, context, query, attended, cot, gain_two, grad_pre, w_in, w_out):
    total = attended.shape[0]
    return pl.pallas_call(
        branch_kernel,
        out_shape=[
            jax.ShapeDtypeStruct((total, D), F32),
            jax.ShapeDtypeStruct((total, D), LOW),
            jax.ShapeDtypeStruct((total, D), LOW),
            jax.ShapeDtypeStruct((8, D), F32),
        ],
        grid_spec=pltpu.PrefetchScalarGridSpec(
            num_scalar_prefetch=1,
            grid=(1,),
            in_specs=[vmem()] * 6 + [hbm()] * 2,
            out_specs=[vmem()] * 4,
            scratch_shapes=[
                pltpu.VMEM((D, FF), LOW),
                pltpu.VMEM((D, D), LOW),
                pltpu.SemaphoreType.DMA((4,)),
                pltpu.VMEM((total, D), F32),
            ],
        ),
        compiler_params=pltpu.CompilerParams(vmem_limit_bytes=28 << 20),
        cost_estimate=SMALL,
        name="branch_grad",
    )(member, context, query, attended, cot, gain_two, grad_pre, w_in, w_out)


def attention_kernel(
    mixed, value, key, scaled_query, weights, o_query, o_key, o_value, o_sums,
    v_weights, sem_in, turned_mixed, turned_key, turned_query, scores, ahead, across, down_query, down_mixed,
):
    total = mixed.shape[0]
    tiles = total // 128
    arrive = Copies(sem_in)
    loads = [arrive.start(weights.at[pair], v_weights.at[pair]) for pair in range(PAIRS)]
    for n in range(3):
        cols = slice(n * 256, (n + 1) * 256)
        turned_mixed[cols, :] = mixed[:, cols].T
        turned_key[cols, :] = key[:, cols].T
    across[...] = jnp.zeros_like(across)
    lane = lax.broadcasted_iota(jnp.int32, (1, 128), 1)
    low_half = (lane < 64).astype(F32).astype(LOW)
    high_half = (lane >= 64).astype(F32).astype(LOW)
    steps = [(pair, t) for pair in range(PAIRS) for t in range(tiles)]

    def parts(pair):
        return slice(pair * 128, pair * 128 + 64), slice(pair * 128 + 64, pair * 128 + 128)

    def spread(i):
        (pair, t), (even, odd) = steps[i], parts(steps[i][0])
        across[i % 2, :64, :128] = turned_mixed[even, t * 128 : (t + 1) * 128]
        across[i % 2, 64:, 128:] = turned_mixed[odd, t * 128 : (t + 1) * 128]
        ahead[i % 2] = product(value[:, pair * 128 : pair * 128 + 128], across[i % 2])

    def weigh(i):
        pair, t = steps[i]
        if t == 0:
            loads[pair].wait()
        chance = v_weights[pair, t].astype(F32)
        both = chance * ahead[i % 2]
        scores[pair % 2, t] = (both - chance * jnp.sum(both, axis=0, keepdims=True)).astype(LOW)

    def gather(i):
        (pair, t), (even, odd) = steps[i], parts(steps[i][0])
        at, cols = slice(pair * 128, pair * 128 + 128), slice(t * 128, (t + 1) * 128)
        part = product(turned_key[at, :], scores[pair % 2, t]) * SCALING
        turned_query[even, cols] = part[:64, :128].astype(LOW)
        turned_query[odd, cols] = part[64:, 128:].astype(LOW)
        for source, target in ((scaled_query, down_query), (mixed, down_mixed)):
            tile = source[cols, at]
            target[t * 256 : t * 256 + 128, :] = tile * low_half
            target[t * 256 + 128 : t * 256 + 256, :] = tile * high_half
        if t == tiles - 1:
            o_key[:, at] = sum(
                product(scores[pair % 2, t], down_query[t * 256 : (t + 1) * 256, :]) for t in range(tiles)
            ).astype(LOW)
            o_value[:, at] = sum(
                product(v_weights[pair, t], down_mixed[t * 256 : (t + 1) * 256, :]) for t in range(tiles)
            ).astype(LOW)

    spread(0)
    for i in range(len(steps)):
        if i + 1 < len(steps):
            spread(i + 1)
        weigh(i)
        if i > 0:
            gather(i - 1)
    gather(len(steps) - 1)
    for n in range(3):
        o_query[:, n * 256 : (n + 1) * 256] = turned_query[n * 256 : (n + 1) * 256, :].T
    o_sums[...] = jnp.zeros_like(o_sums)
    o_sums[0:1, :] = whole(fold(o_query[...].astype(F32)))
    o_sums[1:2, :] = whole(fold(o_value[...].astype(F32)))


def attention_grad(mixed, value, key, scaled_query, weights):
    count, total = value.shape[0], mixed.shape[0]
    return pl.pallas_call(
        attention_kernel,
        out_shape=[
            jax.ShapeDtypeStruct((total, D), LOW),
            jax.ShapeDtypeStruct((count, D), LOW),
            jax.ShapeDtypeStruct((count, D), LOW),
            jax.ShapeDtypeStruct((8, D), F32),
        ],
        in_specs=[vmem()] * 4 + [hbm()],
        out_specs=[vmem()] * 4,
        scratch_shapes=[
            pltpu.VMEM(weights.shape, LOW),
            pltpu.SemaphoreType.DMA((PAIRS,)),
            pltpu.VMEM((D, total), LOW),
            pltpu.VMEM((D, count), LOW),
            pltpu.VMEM((D, total), LOW),
            pltpu.VMEM((2, total // 128, count, 256), LOW),
            pltpu.VMEM((2, count, 256), F32),
            pltpu.VMEM((2, 128, 256), LOW),
            pltpu.VMEM((2 * total, 128), LOW),
            pltpu.VMEM((2 * total, 128), LOW),
        ],
        compiler_params=pltpu.CompilerParams(vmem_limit_bytes=28 << 20),
        cost_estimate=SMALL,
        name="attention_grad",
    )(mixed, value, key, scaled_query, weights)


def input_kernel(
    info, context, query, gain_one, after, grad_query, grad_key, grad_value, w_query, w_key, w_value,
    sums_one, sums_two, sum_in, sum_down, o_far, o_near, o_query, rows_grad, context_grad,
):
    count, fresh = context.shape[0], query.shape[0]
    own = count // 4
    for n in range(3):
        cols = slice(n * 256, (n + 1) * 256)
        rows_grad[:, cols] = transposed_right(grad_query[...], w_query[cols, :])
        context_grad[:, cols] = transposed_right(grad_key[...], w_key[cols, :]) + transposed_right(
            grad_value[...], w_value[cols, :]
        )
    gain = wide(gain_one)
    zero = jnp.zeros((8, D), F32)

    def pull(base, grad, carry):
        standard, inverse = standardize(base.astype(F32))
        one, two = carry
        return norm_pullback(standard, inverse, gain, grad), (one + fold(grad * standard), two + fold(grad))

    carry = (zero, zero)
    for y in range(2):
        for side, target in ((0, o_near), (1, o_far)):

            def one(i, carry):
                at = i * 64
                rows = ds((y * 2 + (info[3] ^ side)) * own + at, 64)
                grad = context_grad[rows, :]
                if side:
                    out, carry = pull(context[rows, :], grad, carry)
                else:
                    mine = info[2] == y
                    grad = grad + jnp.where(mine, rows_grad[ds(at, 64), :], 0.0)
                    out, carry = pull(context[rows, :], grad, carry)
                    out = out + jnp.where(mine, after[ds(at, 64), :], 0.0)
                target[ds(y * own + at, 64), :] = out
                return carry

            carry = lax.fori_loop(0, own // 64, one, carry)

    def rest(i, carry):
        rows = ds(i * 64, 64)
        out, carry = pull(query[rows, :], rows_grad[ds(own + i * 64, 64), :], carry)
        o_query[rows, :] = out + after[ds(own + i * 64, 64), :]
        return carry

    carry = lax.fori_loop(0, fresh // 64, rest, carry)
    for target in (o_near, o_far):
        small = target.at[2 * own :, :]
        small[0:1, :], small[1:2, :] = whole(carry[0]), whole(carry[1])
        small[2:4, :] = sums_two[:2, :]
        small[4:7, :] = sums_one[:3, :]
        small[7:8, :] = sum_down[...]
        for j in range(4):
            small[8 + j : 9 + j, :] = sum_in[:, j * D : (j + 1) * D]
        small[12:, :] = jnp.zeros((4, D), F32)


def input_grad(member, args, own, fresh, count):
    shapes = [(2 * own + 16, D), (2 * own + 16, D), (fresh, D)]
    return pl.pallas_call(
        input_kernel,
        out_shape=[jax.ShapeDtypeStruct(s, F32) for s in shapes],
        grid_spec=pltpu.PrefetchScalarGridSpec(
            num_scalar_prefetch=1,
            grid=(1,),
            in_specs=[vmem()] * len(args),
            out_specs=[vmem()] * 3,
            scratch_shapes=[pltpu.VMEM((own + fresh, D), F32), pltpu.VMEM((count, D), F32)],
        ),
        compiler_params=pltpu.CompilerParams(vmem_limit_bytes=24 << 20),
        cost_estimate=SMALL,
        name="input_grad",
    )(member, *args)


def body(
    context_in,
    query_in,
    context_seg,
    query_seg,
    attn_gain,
    attn_shift,
    w_query,
    b_query,
    w_key,
    w_value,
    b_value,
    w_out,
    b_out,
    mlp_gain,
    mlp_shift,
    w_in,
    b_in,
    w_down,
    b_down,
    context_cot,
    query_cot,
):
    count, fresh = context_in.shape[1], query_in.shape[1]
    seqs = lax.axis_size("seq")
    plan = Plan(seqs, lax.axis_size("qry"))
    own = count // 4
    total = own + fresh
    index, member = plan.member, plan.info
    context, query = context_in[0], query_in[0]
    direct = FF // seqs % 128 == 0
    turn = Turn()

    cot, context_low, rows_low, scaled_query, keys, values, weights, mixed, attended, normed_two, hidden, slope = forward(
        member,
        context,
        query,
        context_seg,
        query_seg,
        (attn_gain, attn_shift, b_query, b_value, b_out, mlp_gain, mlp_shift, b_in),
        (w_query, w_key, w_value, w_out, w_in),
        (context_cot[0], query_cot[0]),
    )
    turn.done(hidden)

    orders = {"down": ("xhyl", "ylhx"), "in": ("xyhl", "yxlh"), "square": ("xyhl", "lxyh")}

    def part(sides, pieces, kernel, name, args, rows, lanes, turned):
        setup = Setup(plan, orders[name], sides, pieces)
        out = block_call(kernel, name + "_grad", plan, setup, turn.wait(*args), rows, lanes, turned)
        turn.done(*out)
        return out

    def scatter(name, *parts):
        return [Scatter(plan, orders[name], *part) for part in parts]

    def spread(name, *products):
        return scatter(name, *[plan.plain(transposed_left(*one), orders[name]) for one in products])

    def step(group):
        for one in group:
            one.step(turn)

    core_pairs = [(q, q ^ 1) for q in range(4)]
    y_pairs = [(q, q ^ 2) for q in range(4)]

    def both(name, pieces, apart, call, products):
        if not direct:
            return spread(name, *products)
        if apart:
            sent = part((1,), pieces, *call)
            return scatter(name, (sent, part((0,), pieces, *call)[0]))
        out = part((1, 0), pieces, *call)
        return scatter(name, (out[:pieces], out[pieces]))

    downs = both("down", 1, True, (down_kernel, "down", (hidden, cot), 192, FF // seqs, [(384, total)]), [(hidden, cot)])
    cot_now, slope_now = turn.wait(cot, slope)
    grad_pre, sum_in, sum_down = hidden_grad(cot_now, w_down, slope_now)
    turn.done(grad_pre)
    step(downs)
    ins = both(
        "in", 4, False, (in_kernel, "in", (normed_two, grad_pre), D // seqs, D, [(D, total)]), [(normed_two, grad_pre)]
    )
    (grad_pre_now,) = turn.wait(grad_pre)
    grad_after, branch, grad_mixed, sums_one = branch_grad(
        member, context, query, attended, cot, mlp_gain, grad_pre_now, w_in, w_out
    )
    turn.done(grad_mixed)
    step(ins)
    (grad_mixed_now,) = turn.wait(grad_mixed)
    grad_query, grad_keys, grad_values, sums_two = attention_grad(
        grad_mixed_now, values, keys, scaled_query, weights
    )
    turn.done(grad_query)
    step(downs)
    squares = both(
        "square",
        2,
        False,
        (
            square_kernel,
            "square",
            (context_low, rows_low, mixed, grad_keys, grad_values, grad_query, branch),
            2 * D // seqs,
            384,
            [(D, count), (D, total), (D, total)],
        ),
        [(context_low, grad_keys), (context_low, grad_values), (rows_low, grad_query), (mixed, branch)],
    )
    (grad_query_now,) = turn.wait(grad_query)
    far, near, query_grad = input_grad(
        member,
        (
            context, query, attn_gain, grad_after, grad_query_now, grad_keys, grad_values,
            w_query, w_key, w_value, sums_one, sums_two, sum_in, sum_down,
        ),
        own,
        fresh,
        count,
    )
    turn.done(query_grad)
    received = lax.ppermute(far, "qry", core_pairs)
    step(ins)
    step(squares)
    step(downs)
    near, received = turn.wait(near, received)
    pair = near + received
    turn.done(pair)
    pair_far = lax.ppermute(pair, "qry", y_pairs)
    (hidden_now,) = turn.wait(hidden)
    added = attended + product(hidden_now, w_down) + b_down.astype(F32)
    turn.done(added)
    out_far = lax.ppermute(added[:own], "qry", y_pairs)

    def small_step(bit, last=False):
        nonlocal small, small_far
        if bit:
            small, small_far = turn.wait(small, small_far)
            small = small + small_far
            turn.done(small)
        if not last:
            small_far = lax.ppermute(small, "seq", [(s, s ^ (1 << bit)) for s in range(seqs)])

    step(downs)
    step(ins)
    added_own, out_far = turn.wait(added[:own], out_far)
    first = plan.y == 0
    out_pair = jnp.stack([jnp.where(first, added_own, out_far), jnp.where(first, out_far, added_own)])
    turn.done(out_pair)
    out_near = lax.ppermute(out_pair, "qry", core_pairs)
    step(squares)
    pair, pair_far = turn.wait(pair, pair_far)
    grad_pair = (pair[: 2 * own] + pair_far[: 2 * own]).reshape(2, own, D)
    small, small_far = pair[2 * own :] + pair_far[2 * own :], None
    turn.done(grad_pair, small)
    grad_near = lax.ppermute(grad_pair, "qry", core_pairs)
    small_step(0)
    grad_down = downs[0].finish(turn)
    if direct:
        grad_down = grad_down.T
    step(ins)
    small_step(1)
    step(squares)
    small_step(2)
    grad_in = ins[0].finish(turn)
    for bit in range(3, plan.bits):
        small_step(bit)
    step(squares)
    small_step(plan.bits, True)
    square = [one.finish(turn) for one in squares]
    if direct:
        height = D // seqs
        grad_w_key, grad_w_value = square[0][:height, :192], square[0][:height, 192:]
        grad_w_query, grad_w_out = square[0][height:, :192], square[0][height:, 192:]
    else:
        grad_w_key, grad_w_value, grad_w_query, grad_w_out = square

    def place(pair, near):
        low = plan.core == 0
        one, two = jnp.where(low, pair, near), jnp.where(low, near, pair)
        return jnp.stack([one, two], axis=1).reshape(count, D)

    context_grad = place(grad_pair, grad_near)
    context_out = (context.astype(F32) + place(out_pair, out_near)).astype(LOW)
    query_out = (query.astype(F32) + added[own:]).astype(LOW)
    return (
        context_out[None],
        query_out[None],
        context_grad[None],
        query_grad[None],
        small[0],
        small[1],
        grad_w_query,
        small[2],
        grad_w_key,
        grad_w_value,
        small[3],
        grad_w_out,
        small[4],
        small[5],
        small[6],
        grad_in,
        small[8:12].reshape(-1),
        grad_down,
        small[7],
    )


def solution(mesh):
    placed = (
        P("seq", None, None),
        P("seq", "qry", None),
        P("seq", None),
        P("seq", "qry"),
        P(),
        P(),
        P(),
        P(),
        P(),
        P(),
        P(),
        P(),
        P(),
        P(),
        P(),
        P(),
        P(),
        P(),
        P(),
        P("seq", None, None),
        P("seq", "qry", None),
    )
    return jax.shard_map(
        body,
        mesh=mesh,
        in_specs=placed,
        out_specs=(
            P("seq", None, None),
            P("seq", "qry", None),
            P("seq", None, None),
            P("seq", "qry", None),
            P(),
            P(),
            P("seq", "qry"),
            P(),
            P("seq", "qry"),
            P("seq", "qry"),
            P(),
            P("seq", "qry"),
            P(),
            P(),
            P(),
            P("seq", "qry"),
            P(),
            P("seq", "qry"),
            P(),
        ),
        check_vma=False,
    )
```

```python
import functools

import jax
import jax.numpy as jnp
from jax import lax
from jax.experimental import pallas as pl
from jax.experimental.pallas import tpu as pltpu
from jax.sharding import PartitionSpec as P

D = 768
HEADS = 12
HEAD_DIM = 64
FF = 3072
PAIRS = HEADS // 2

EPSILON = 1e-05
MASKED = -1e30
LOW = jnp.bfloat16
F32 = jnp.float32
SCALING = HEAD_DIM ** (-0.5)
BEND = 0.7978845608028654
CUBE = 0.044715 * BEND


def standardize(values):
    center = values - jnp.mean(values, axis=-1, keepdims=True)
    spread = jnp.mean(center * center, axis=-1, keepdims=True)
    inverse = lax.rsqrt(spread + EPSILON)
    return center * inverse, inverse


def norm_pullback(standard, inverse, gain, grad):
    scaled = grad * gain
    first = jnp.mean(scaled, axis=-1, keepdims=True)
    second = jnp.mean(scaled * standard, axis=-1, keepdims=True)
    return inverse * (scaled - first - standard * second)


def product(left, right):
    return jnp.dot(left, right, preferred_element_type=F32)


def transposed_left(left, right):
    return lax.dot_general(left, right, (((0,), (0,)), ((), ())), preferred_element_type=F32)


def transposed_right(left, right):
    return lax.dot_general(left, right, (((1,), (1,)), ((), ())), preferred_element_type=F32)


def wide(ref):
    return ref[...].astype(F32).reshape(1, -1)


def ds(start, size):
    return pl.ds(pl.multiple_of(start, size), size)


def fold(values):
    return jnp.sum(values.reshape(values.shape[0] // 8, 8, values.shape[1]), axis=0)


def whole(values):
    return jnp.sum(values, axis=0, keepdims=True)


def vmem():
    return pl.BlockSpec(memory_space=pltpu.VMEM)


def hbm():
    return pl.BlockSpec(memory_space=pltpu.HBM)


SMALL = pl.CostEstimate(flops=0, bytes_accessed=0, transcendentals=0)


LIMIT = 28

ORDERS = {
    "down": ("lyxh", "xlyh"),
    "in": ("yhxl", "xlyh"),
    "keys": ("xlyh", "lxyh"),
    "rows": ("yxlh", "xyhl"),
}
SCRIPT = (
    "hid", "D", "in", "br", "I", "att", "D", "sq", "inp", "tI", "K", "R", "I", "D", "ctx", "K", "R",
    "D", "out", "I", "R", "K", "grad", "fD", "sm", "I", "op", "cg", "sm", "R", "K", "co", "sm", "fI",
    "fR", "fK",
)


def after(tokens, kernel, specs, args):
    at = len(args)

    def ordered(*refs):
        return kernel(*refs[:at], *refs[at + len(tokens) :])

    return ordered, list(specs) + [hbm()] * len(tokens), tuple(args) + tuple(tokens)


class Copies:
    def __init__(self, sems):
        self.sems, self.all = sems, []

    def start(self, source, target):
        copy = pltpu.make_async_copy(source, target, self.sems.at[len(self.all)])
        copy.start()
        self.all.append(copy)
        return copy

    def wait(self):
        for copy in self.all:
            copy.wait()


class Plan:
    def __init__(self, seqs, members):
        assert members == 4 and seqs & (seqs - 1) == 0 and seqs >= 8
        self.seqs = seqs
        self.bits = seqs.bit_length() - 1
        self.stages = self.bits + 1
        self.blocks = 2 * seqs
        self.s = lax.axis_index("seq")
        self.member = lax.axis_index("qry")
        self.y, self.core = self.member // 2, self.member % 2
        self.info = jnp.stack([self.member, self.s, self.y, self.core]).astype(jnp.int32)

    def order(self, letters):
        return ["y" if letter == "y" else "xlh".index(letter) for letter in letters] + list(range(3, self.bits))

    def pairs(self, orders, step):
        out = []
        for s in range(self.seqs):
            for y in range(2):
                for core in range(2):
                    bit = self.order(orders[core])[step]
                    to = (s, y ^ 1) if bit == "y" else (s ^ (1 << bit), y)
                    out.append((s * 4 + y * 2 + core, to[0] * 4 + to[1] * 2 + core))
        return out

    def plain(self, grad, orders):
        rows, columns = grad.shape
        tail = (rows // self.seqs, columns // 4)
        parts = grad.reshape(self.seqs, tail[0], 2, 2, tail[1]).transpose(3, 0, 2, 1, 4)
        parts = parts.reshape((2,) + (2,) * self.stages + tail)
        own = {bit: (self.s >> bit) & 1 for bit in range(self.bits)} | {"y": self.y}
        axis = {bit: self.bits - bit for bit in range(self.bits)} | {"y": self.stages}
        for bit in own:
            parts = jnp.where(own[bit] == 1, jnp.flip(parts, axis[bit]), parts)
        both = [
            parts[core].transpose(*[axis[bit] - 1 for bit in self.order(orders[core])], self.stages, self.stages + 1)
            for core in range(2)
        ]
        parts = jnp.stack(both).reshape(2, self.blocks, *tail)
        kept = lax.dynamic_index_in_dim(parts, self.core, 0, keepdims=False)
        sent = lax.dynamic_index_in_dim(parts, 1 - self.core, 0, keepdims=False)
        return [sent], kept


def place_of(order, info, s, y):
    place = 0
    for step, bit in enumerate(order):
        one = (info[2] ^ y) if bit == "y" else ((info[1] ^ s) >> bit) & 1
        place = place + (one << (len(order) - 1 - step))
    return place


class Scatter:
    def __init__(self, plan, orders, sent, kept):
        self.plan, self.orders, self.stage = plan, orders, 0
        pairs = [(q, q ^ 1) for q in range(4)]
        self.terms = [kept] + [lax.ppermute(piece, "qry", pairs) for piece in sent]
        self.pieces = len(sent)

    def step(self, turn):
        plan = self.plan
        if self.stage == plan.stages:
            return
        self.terms = turn.wait(*self.terms)
        half = plan.blocks >> (self.stage + 1)
        leaving = self.sum(half, 2 * half)
        turn.done(leaving)
        self.terms = self.terms + [lax.ppermute(leaving, ("seq", "qry"), plan.pairs(self.orders, self.stage))]
        self.stage += 1

    def touch(self, turn):
        self.terms = turn.wait(*self.terms)
        turn.done(self.terms[-1])

    def sum(self, low, high):
        size = self.plan.blocks // self.pieces
        span = [self.terms[1 + i] for i in range(low // size, -(-high // size))]
        near = span[0][low % size : low % size + high - low] if len(span) == 1 else jnp.concatenate(span, axis=0)
        return functools.reduce(lambda a, b: a + b, [t[low:high] for t in self.terms[1 + self.pieces :]], self.terms[0][low:high] + near)

    def finish(self, turn):
        while self.stage < self.plan.stages:
            self.step(turn)
        self.terms = turn.wait(*self.terms)
        out = self.sum(0, 1)[0]
        turn.done(out)
        return out


class Turn:
    def __init__(self):
        self.last = []

    def wait(self, *values):
        if self.last:
            out = lax.optimization_barrier((*values, *self.last))
            values = out[: len(values)]
        return list(values)

    def done(self, *values):
        self.last = list(values)


def pick(ref, y, half):
    low = ref[:, y * 384 : y * 384 + 192]
    high = ref[:, y * 384 + 192 : y * 384 + 384]
    return jnp.where(half == 0, low, high)


def in_kernel(setup, info, normed, grad, *rest):
    seqs, outs, (turned, stage, sems) = setup.seqs, rest[: setup.outs], rest[setup.outs :]
    turned[...] = normed[...].T
    height = D // seqs
    leaves = []
    for side, half in setup.halves(info):
        leave = Blocks(setup, side, outs, sems)
        for y in range(2):
            start = pl.multiple_of((y * 2 + half) * D, 128)
            for n in range(3):
                part = product(turned[...], grad[:, pl.ds(pl.multiple_of(start + n * 256, 128), 256)])
                for s in range(seqs):
                    stage[leave.at(s, y), :, n * 256 : (n + 1) * 256] = part[s * height : (s + 1) * height]
            for s in range(seqs):
                leave.start(stage, leave.at(s, y), setup.place(half, info, s, y))
        leaves.append(leave)
    for leave in leaves:
        leave.wait(stage)


def square_kernel(setups, info, normed_context, normed, mixed, gk, gv, gq, ga, *rest):
    outs, (turned_c, turned_a, turned_o, *more) = rest[:4], rest[4:]
    turned_c[...] = normed_context[...].T
    turned_a[...] = normed[...].T
    turned_o[...] = mixed[...].T
    height = D // setups[0].seqs
    leaves = []
    for side in range(2):
        for which, setup in enumerate(setups):
            _, half = setup.halves(info)[side]
            stage, sems = more[2 * which : 2 * which + 2]
            leave = Blocks(setup, side, outs[2 * which : 2 * which + 2], sems)
            for y in range(2):
                if which == 0:
                    part = product(turned_c[...], jnp.concatenate([pick(gk, y, half), pick(gv, y, half)], axis=1))
                else:
                    part = jnp.concatenate(
                        [product(turned_a[...], pick(gq, y, half)), product(turned_o[...], pick(ga, y, half))], axis=1
                    )
                for s in range(setup.seqs):
                    stage[leave.at(s, y)] = part[s * height : (s + 1) * height]
                    leave.start(stage, leave.at(s, y), setup.place(half, info, s, y))
            leaves.append((leave, stage))
    for leave, stage in leaves:
        leave.wait(stage)


def square_call(plan, setups, args):
    blocks = plan.blocks
    rows = D // plan.seqs
    return pl.pallas_call(
        functools.partial(square_kernel, setups),
        out_shape=[pltpu.HBM((blocks, rows, 384), F32)] * 4,
        grid_spec=pltpu.PrefetchScalarGridSpec(
            num_scalar_prefetch=1,
            grid=(1,),
            in_specs=[vmem()] * len(args),
            out_specs=[hbm()] * 4,
            scratch_shapes=[pltpu.VMEM((D, a.shape[0]), LOW) for a in args[:3]]
            + [pltpu.VMEM((2 * blocks, rows, 384), F32), pltpu.SemaphoreType.DMA((2 * blocks,))] * 2,
        ),
        compiler_params=pltpu.CompilerParams(vmem_limit_bytes=LIMIT << 20),
        cost_estimate=SMALL,
        name="square_grad",
    )(plan.info, *args)


class Setup:
    def __init__(self, plan, orders, sides, pieces):
        self.seqs, self.sides, self.pieces = plan.seqs, sides, pieces
        self.orders = [plan.order(letters) for letters in orders]
        self.blocks = plan.blocks
        self.counts = [pieces if side else 1 for side in sides]
        self.outs = sum(self.counts)

    def halves(self, info):
        return [(i, info[3] ^ side) for i, side in enumerate(self.sides)]

    def place(self, half, info, s, y):
        one, two = [place_of(order, info, s, y) for order in self.orders]
        return jnp.where(half == 0, one, two)


class Blocks:
    def __init__(self, setup, side, outs, sems):
        before = sum(setup.counts[:side])
        self.outs, self.sems, self.all = outs[before : before + setup.counts[side]], sems, []
        self.first, self.seqs = side * setup.blocks, setup.seqs

    def at(self, s, y):
        return self.first + s * 2 + y

    def each(self, stage, at, place, act):
        size = self.outs[0].shape[0]
        if len(self.outs) == 1:
            act(pltpu.make_async_copy(stage.at[at], self.outs[0].at[place], self.sems.at[at]))
            return
        for i, out in enumerate(self.outs):

            @pl.when((place >= i * size) & (place < (i + 1) * size))
            def _():
                act(pltpu.make_async_copy(stage.at[at], out.at[place - i * size], self.sems.at[at]))

    def start(self, stage, at, place):
        self.all.append((at, place))
        self.each(stage, at, place, lambda copy: copy.start())

    def wait(self, stage):
        for at, place in self.all:
            self.each(stage, at, place, lambda copy: copy.wait())


def block_call(kernel, name, plan, setup, args, rows, lanes, turned):
    blocks = plan.blocks * len(setup.sides)
    shapes = []
    for count in setup.counts:
        shapes += [pltpu.HBM((plan.blocks // count, rows, lanes), F32)] * count
    return pl.pallas_call(
        functools.partial(kernel, setup),
        out_shape=shapes,
        grid_spec=pltpu.PrefetchScalarGridSpec(
            num_scalar_prefetch=1,
            grid=(1,),
            in_specs=[vmem()] * len(args),
            out_specs=[hbm()] * len(shapes),
            scratch_shapes=[pltpu.VMEM(t, LOW) for t in turned]
            + [pltpu.VMEM((blocks, rows, lanes), F32), pltpu.SemaphoreType.DMA((blocks,))],
        ),
        compiler_params=pltpu.CompilerParams(vmem_limit_bytes=LIMIT << 20),
        cost_estimate=SMALL,
        name=name,
    )(plan.info, *args)


def forward_kernel(
    setup, info, context, query, context_seg, query_seg, gain_one, shift_one, b_query, b_value, b_out, gain_two, shift_two, b_in,
    w_query, w_key, w_value, w_out, w_in, context_cot, query_cot,
    *rest,
):
    names = 12
    outs, rest = rest[:names], rest[names:]
    o_cot, o_context, o_rows, o_query, o_key, o_value, o_weights, o_mixed, o_attended, o_normed, o_hidden, o_slope = outs
    if setup:
        o_down, rest = rest[:2], rest[2:]
    v_wq, v_wk, v_wv, v_wo, v_win, sem_in, *rest = rest
    scratch, rest = rest[:names], rest[names:]
    s_cot, s_context, s_rows, s_query, s_key, s_value, s_weights, s_mixed, s_attended, s_normed, s_hidden, s_slope = scratch
    turned_query, turned_value, turned_mixed, bias, diag, scores, ahead, sem_out, *rest = rest
    if setup:
        turned_cot, stage, sem_down = rest
    count, fresh = context.shape[0], query.shape[0]
    total = s_rows.shape[0]
    own = total - fresh
    tiles = total // 128
    arrive = Copies(sem_in)
    loads = [
        arrive.start(source, target)
        for source, target in [
            (w_query, v_wq),
            (w_key, v_wk),
            (w_value, v_wv),
            (w_out, v_wo),
            (w_in, v_win),
            (context_cot.at[ds(info[0] * own, own), :], s_cot.at[:own, :]),
            (query_cot, s_cot.at[own:, :]),
        ]
    ]
    leave = Copies(sem_out)
    send = leave.start
    gain, shift = wide(gain_one), wide(shift_one)

    def normalize(source, target, at, step):
        def one(i, carry):
            rows = pl.ds(pl.multiple_of(i * step, step), step)
            standard, _ = standardize(source[rows, :].astype(F32))
            target[pl.ds(pl.multiple_of(at + i * step, step), step), :] = (standard * gain + shift).astype(LOW)
            return carry
        lax.fori_loop(0, source.shape[0] // step, one, 0)

    normalize(context, s_context, 0, 64)
    normalize(query, s_rows, own, 64)
    s_rows[:own, :] = s_context[pl.ds(pl.multiple_of(info[0] * own, own), own), :]
    send(s_context, o_context)
    send(s_rows, o_rows)

    keys = jnp.broadcast_to(context_seg[...].astype(F32), (128, count)).T
    for t in range(tiles):
        if t * 128 < own:
            rows = context_seg[:, pl.ds(pl.multiple_of(info[0] * own + t * 128, 128), 128)]
        else:
            rows = query_seg[:, t * 128 - own : t * 128 - own + 128]
        bias[:, t * 128 : (t + 1) * 128] = jnp.where(keys == rows.astype(F32), 0.0, MASKED)

    loads[0].wait()
    for n in range(3):
        cols = slice(n * 256, (n + 1) * 256)
        part = product(s_rows[...], v_wq[:, cols]) + b_query[cols].astype(F32).reshape(1, -1)
        part = (part.astype(LOW) * jnp.asarray(SCALING, LOW))
        s_query[:, cols] = part
        turned_query[cols, :] = part.T
    send(s_query, o_query)
    loads[1].wait()
    for n in range(3):
        cols = slice(n * 256, (n + 1) * 256)
        s_key[:, cols] = product(s_context[...], v_wk[:, cols]).astype(LOW)
    send(s_key, o_key)
    loads[2].wait()
    for n in range(3):
        cols = slice(n * 256, (n + 1) * 256)
        part = (product(s_context[...], v_wv[:, cols]) + b_value[cols].astype(F32).reshape(1, -1)).astype(LOW)
        s_value[:, cols] = part
        turned_value[cols, :] = part.T
    send(s_value, o_value)
    loads[5].wait()
    loads[6].wait()
    send(s_cot, o_cot)

    diag[...] = jnp.zeros_like(diag)

    steps = [(pair, t) for pair in range(PAIRS) for t in range(tiles)]

    def parts(pair):
        return slice(pair * 128, pair * 128 + 64), slice(pair * 128 + 64, pair * 128 + 128)

    def score(i):
        (pair, t), (even, odd) = steps[i], parts(steps[i][0])
        diag[i % 2, :64, :128] = turned_query[even, t * 128 : (t + 1) * 128]
        diag[i % 2, 64:, 128:] = turned_query[odd, t * 128 : (t + 1) * 128]
        scores[i % 2] = product(s_key[:, pair * 128 : pair * 128 + 128], diag[i % 2])

    def weigh(i):
        pair, t = steps[i]
        for side in range(2):
            lanes = slice(side * 128, (side + 1) * 128)
            part = scores[i % 2, :, lanes] + bias[:, t * 128 : (t + 1) * 128]
            raised = jnp.exp(part - jnp.max(part, axis=0, keepdims=True))
            scale = 1.0 / jnp.sum(raised, axis=0, keepdims=True)
            s_weights[pair, t, :, lanes] = (raised * scale).astype(LOW)

    def mix(i):
        (pair, t), (even, odd) = steps[i], parts(steps[i][0])
        both = product(turned_value[pair * 128 : pair * 128 + 128, :], s_weights[pair, t])
        turned_mixed[even, t * 128 : (t + 1) * 128] = both[:64, :128].astype(LOW)
        turned_mixed[odd, t * 128 : (t + 1) * 128] = both[64:, 128:].astype(LOW)
        if t == tiles - 1:
            send(s_weights.at[pair], o_weights.at[pair])

    score(0)
    for i in range(len(steps)):
        if i + 1 < len(steps):
            score(i + 1)
        weigh(i)
        if i > 0:
            mix(i - 1)
    mix(len(steps) - 1)
    for n in range(3):
        s_mixed[:, n * 256 : (n + 1) * 256] = turned_mixed[n * 256 : (n + 1) * 256, :].T
    send(s_mixed, o_mixed)
    loads[3].wait()
    for n in range(3):
        cols = slice(n * 256, (n + 1) * 256)
        s_attended[:, cols] = product(s_mixed[...], v_wo[:, cols]) + b_out[cols].astype(F32).reshape(1, -1)
    send(s_attended, o_attended)
    gain, shift = wide(gain_two), wide(shift_two)

    def second(i, carry):
        rows = pl.ds(pl.multiple_of(i * 64, 64), 64)

        def put(base):
            standard, _ = standardize(base.astype(F32) + s_attended[rows, :])
            s_normed[rows, :] = (standard * gain + shift).astype(LOW)

        @pl.when(i < own // 64)
        def _():
            put(context[pl.ds(pl.multiple_of(info[0] * own + i * 64, 64), 64), :])

        @pl.when(i >= own // 64)
        def _():
            put(query[pl.ds(pl.multiple_of(i * 64 - own, 64), 64), :])

        return carry

    lax.fori_loop(0, total // 64, second, 0)
    send(s_normed, o_normed)
    loads[4].wait()
    steps = FF // 256
    if setup:
        width, ready = FF // setup.seqs, 0
        downs = [Blocks(setup, side, o_down, sem_down) for side in range(2)]
        halves = [half for _, half in setup.halves(info)]
        for side, half in enumerate(halves):
            for y in range(2):
                at = (side * 2 + y) * 192
                turned_cot[at : at + 192, :] = pick(s_cot, y, half).T
    ahead[0] = product(s_normed[...], v_win[:, :256])
    for n in range(steps):
        cols = slice(n * 256, (n + 1) * 256)
        if n + 1 < steps:
            ahead[(n + 1) % 2] = product(s_normed[...], v_win[:, (n + 1) * 256 : (n + 2) * 256])
        extra = b_in[cols].astype(F32).reshape(1, -1)
        for m in range(total // 64):
            rows = slice(m * 64, (m + 1) * 64)
            h = ahead[n % 2, rows, :] + extra
            square = h * h
            t = jnp.tanh(h * (BEND + CUBE * square))
            part = 0.5 + 0.5 * t
            s_hidden[rows, cols] = (h * part).astype(LOW)
            bend = h * (BEND + 3 * CUBE * square)
            s_slope[rows, cols] = (part * (1.0 + bend * (1.0 - t))).astype(LOW)
        send(s_hidden.at[:, cols], o_hidden.at[:, cols])
        send(s_slope.at[:, cols], o_slope.at[:, cols])
        while setup and (ready + 1) * width <= (n + 1) * 256:
            part = product(turned_cot[...], s_hidden[:, ready * width : (ready + 1) * width])
            for side, half in enumerate(halves):
                for y in range(2):
                    at = downs[side].at(ready, y)
                    stage[at] = part[(side * 2 + y) * 192 : (side * 2 + y + 1) * 192]
                    downs[side].start(stage, at, setup.place(half, info, ready, y))
            ready += 1
    if setup:
        for down in downs:
            down.wait(stage)
    leave.wait()

def forward(plan, setup, context, query, context_seg, query_seg, vectors, weights, cots):
    count, fresh = context.shape[0], query.shape[0]
    own = count // 4
    total = own + fresh
    kept = [
        ((total, D), LOW),
        ((count, D), LOW),
        ((total, D), LOW),
        ((total, D), LOW),
        ((count, D), LOW),
        ((count, D), LOW),
        ((PAIRS, total // 128, count, 256), LOW),
        ((total, D), LOW),
        ((total, D), F32),
        ((total, D), LOW),
        ((total, FF), LOW),
        ((total, FF), LOW),
    ]
    block = (plan.blocks, 192, FF // plan.seqs)
    return pl.pallas_call(
        functools.partial(forward_kernel, setup),
        out_shape=[jax.ShapeDtypeStruct(*s) for s in kept] + ([pltpu.HBM(block, F32)] * 2 if setup else []),
        grid_spec=pltpu.PrefetchScalarGridSpec(
            num_scalar_prefetch=1,
            grid=(1,),
            in_specs=[vmem()] * 12 + [hbm()] * 7,
            out_specs=[hbm()] * (len(kept) + 2 * bool(setup)),
            scratch_shapes=[pltpu.VMEM((D, D), LOW)] * 4
            + [pltpu.VMEM((D, FF), LOW), pltpu.SemaphoreType.DMA((7,))]
            + [pltpu.VMEM(*s) for s in kept]
            + [
                pltpu.VMEM((D, total), LOW),
                pltpu.VMEM((D, count), LOW),
                pltpu.VMEM((D, total), LOW),
                pltpu.VMEM((count, total), F32),
                pltpu.VMEM((2, 128, 256), LOW),
                pltpu.VMEM((2, count, 256), F32),
                pltpu.VMEM((2, total, 256), F32),
                pltpu.SemaphoreType.DMA((9 + PAIRS + 2 * FF // 256,)),
            ]
            + (
                [
                    pltpu.VMEM((D, total), LOW),
                    pltpu.VMEM((2 * block[0], *block[1:]), F32),
                    pltpu.SemaphoreType.DMA((2 * plan.blocks,)),
                ]
                if setup
                else []
            ),
        ),
        compiler_params=pltpu.CompilerParams(vmem_limit_bytes=58 << 20),
        cost_estimate=SMALL,
        name="forward",
    )(plan.info, context, query, context_seg, query_seg, *vectors, *weights, *cots)


def hidden_kernel(cot, w_down, slope, out, sum_in, sum_down):
    for n in range(w_down.shape[0] // 256):
        cols = slice(n * 256, (n + 1) * 256)
        out[:, cols] = (transposed_right(cot[...], w_down[cols, :]) * slope[:, cols].astype(F32)).astype(LOW)
    sum_in[...] = whole(fold(out[...].astype(F32)))

    @pl.when(pl.program_id(0) == 0)
    def _():
        sum_down[...] = whole(fold(cot[...].astype(F32)))


def hidden_grad(cot, w_down, slope):
    total, step = cot.shape[0], 768
    return pl.pallas_call(
        hidden_kernel,
        out_shape=[
            jax.ShapeDtypeStruct((total, FF), LOW),
            jax.ShapeDtypeStruct((1, FF), F32),
            jax.ShapeDtypeStruct((1, D), F32),
        ],
        grid=(FF // step,),
        in_specs=[
            pl.BlockSpec((total, D), lambda i: (0, 0)),
            pl.BlockSpec((step, D), lambda i: (i, 0)),
            pl.BlockSpec((total, step), lambda i: (0, i)),
        ],
        out_specs=[
            pl.BlockSpec((total, step), lambda i: (0, i)),
            pl.BlockSpec((1, step), lambda i: (0, i)),
            pl.BlockSpec((1, D), lambda i: (0, 0)),
        ],
        compiler_params=pltpu.CompilerParams(vmem_limit_bytes=16 << 20),
        cost_estimate=SMALL,
        name="hidden_grad",
    )(cot, w_down, slope)


def small_kernel(left, right, out):
    out[...] = left[...] + right[...]


def add_small(tokens, left, right):
    kernel, specs, args = after(tokens, small_kernel, [vmem()] * 2, (left, right))
    return pl.pallas_call(
        kernel,
        out_shape=jax.ShapeDtypeStruct(left.shape, F32),
        in_specs=specs,
        out_specs=vmem(),
        cost_estimate=SMALL,
        name="add_small",
    )(*args)


def output_kernel(hidden, w_down, attended, query, b_down, o_added, o_query, added):
    step, last = pl.program_id(0), pl.num_programs(0) - 1
    own = o_added.shape[0]

    @pl.when(step == 0)
    def _():
        added[...] = attended[...] + wide(b_down)

    for n in range(3):
        cols = slice(n * 256, (n + 1) * 256)
        added[:, cols] += product(hidden[...], w_down[:, cols])

    @pl.when(step == last)
    def _():
        o_added[...] = added[:own, :]
        o_query[...] = (query[...].astype(F32) + added[own:, :]).astype(LOW)


def outputs(tokens, hidden, w_down, attended, query, b_down):
    total, fresh, step = hidden.shape[0], query.shape[0], 1536
    fixed = lambda rows: pl.BlockSpec((rows, D), lambda i: (0, 0))
    specs = [
        pl.BlockSpec((total, step), lambda i: (0, i)),
        pl.BlockSpec((step, D), lambda i: (i, 0)),
        fixed(total),
        fixed(fresh),
        pl.BlockSpec((D,), lambda i: (0,)),
    ]
    kernel, specs, args = after(tokens, output_kernel, specs, (hidden, w_down, attended, query, b_down))
    return pl.pallas_call(
        kernel,
        out_shape=[
            jax.ShapeDtypeStruct((total - fresh, D), F32),
            jax.ShapeDtypeStruct((fresh, D), LOW),
        ],
        grid_spec=pltpu.PrefetchScalarGridSpec(
            num_scalar_prefetch=0,
            grid=(FF // step,),
            in_specs=specs,
            out_specs=[fixed(total - fresh), fixed(fresh)],
            scratch_shapes=[pltpu.VMEM((total, D), F32)],
        ),
        compiler_params=pltpu.CompilerParams(vmem_limit_bytes=58 << 20),
        cost_estimate=SMALL,
        name="outputs",
    )(*args)


def branch_kernel(
    info, context, query, attended, cot, gain_two, grad_pre, w_in, w_out,
    o_after, o_branch, o_mixed, o_sums,
    v_win, v_wout, sem_in, normed,
):
    total, fresh = attended.shape[0], query.shape[0]
    own = total - fresh
    arrive = Copies(sem_in)
    loads = [arrive.start(w_in.at[n * 256 : (n + 1) * 256, :], v_win.at[n * 256 : (n + 1) * 256, :]) for n in range(3)]
    last = arrive.start(w_out, v_wout)
    for n in range(3):
        cols = slice(n * 256, (n + 1) * 256)
        loads[n].wait()
        normed[:, cols] = transposed_right(grad_pre[...], v_win[cols, :])
    gain = wide(gain_two)

    def back(i, carry, base):
        rows = ds(i * 32, 32)
        standard, inverse = standardize(base.astype(F32) + attended[rows, :])
        grad = normed[rows, :]
        after = cot[rows, :].astype(F32) + norm_pullback(standard, inverse, gain, grad)
        o_after[rows, :] = after
        low = after.astype(LOW)
        o_branch[rows, :] = low
        one, two, three = carry
        return one + fold(grad * standard), two + fold(grad), three + fold(low.astype(F32))

    zero = jnp.zeros((8, D), F32)
    sums = lax.fori_loop(
        0, own // 32, lambda i, c: back(i, c, context[ds(info[0] * own + i * 32, 32), :]), (zero, zero, zero)
    )
    sums = lax.fori_loop(own // 32, total // 32, lambda i, c: back(i, c, query[ds(i * 32 - own, 32), :]), sums)
    o_sums[...] = jnp.zeros_like(o_sums)
    o_sums[0:1, :], o_sums[1:2, :], o_sums[2:3, :] = whole(sums[2]), whole(sums[0]), whole(sums[1])
    last.wait()
    for n in range(3):
        cols = slice(n * 256, (n + 1) * 256)
        o_mixed[:, cols] = transposed_right(o_branch[...], v_wout[cols, :]).astype(LOW)


def branch_grad(member, context, query, attended, cot, gain_two, grad_pre, w_in, w_out):
    total = attended.shape[0]
    return pl.pallas_call(
        branch_kernel,
        out_shape=[
            jax.ShapeDtypeStruct((total, D), F32),
            jax.ShapeDtypeStruct((total, D), LOW),
            jax.ShapeDtypeStruct((total, D), LOW),
            jax.ShapeDtypeStruct((8, D), F32),
        ],
        grid_spec=pltpu.PrefetchScalarGridSpec(
            num_scalar_prefetch=1,
            grid=(1,),
            in_specs=[vmem()] * 6 + [hbm()] * 2,
            out_specs=[vmem()] * 4,
            scratch_shapes=[
                pltpu.VMEM((D, FF), LOW),
                pltpu.VMEM((D, D), LOW),
                pltpu.SemaphoreType.DMA((4,)),
                pltpu.VMEM((total, D), F32),
            ],
        ),
        compiler_params=pltpu.CompilerParams(vmem_limit_bytes=28 << 20),
        cost_estimate=SMALL,
        name="branch_grad",
    )(member, context, query, attended, cot, gain_two, grad_pre, w_in, w_out)


def attention_kernel(
    mixed, value, key, scaled_query, weights, o_query, o_key, o_value, o_sums,
    v_weights, sem_in, turned_mixed, turned_key, turned_query, scores, ahead, across, down_query, down_mixed,
):
    total = mixed.shape[0]
    tiles = total // 128
    arrive = Copies(sem_in)
    loads = [arrive.start(weights.at[pair], v_weights.at[pair]) for pair in range(PAIRS)]
    for n in range(3):
        cols = slice(n * 256, (n + 1) * 256)
        turned_mixed[cols, :] = mixed[:, cols].T
        turned_key[cols, :] = key[:, cols].T
    across[...] = jnp.zeros_like(across)
    lane = lax.broadcasted_iota(jnp.int32, (1, 128), 1)
    low_half = (lane < 64).astype(F32).astype(LOW)
    high_half = (lane >= 64).astype(F32).astype(LOW)
    steps = [(pair, t) for pair in range(PAIRS) for t in range(tiles)]

    def parts(pair):
        return slice(pair * 128, pair * 128 + 64), slice(pair * 128 + 64, pair * 128 + 128)

    def spread(i):
        (pair, t), (even, odd) = steps[i], parts(steps[i][0])
        across[i % 2, :64, :128] = turned_mixed[even, t * 128 : (t + 1) * 128]
        across[i % 2, 64:, 128:] = turned_mixed[odd, t * 128 : (t + 1) * 128]
        ahead[i % 2] = product(value[:, pair * 128 : pair * 128 + 128], across[i % 2])

    def weigh(i):
        pair, t = steps[i]
        if t == 0:
            loads[pair].wait()
        chance = v_weights[pair, t].astype(F32)
        both = chance * ahead[i % 2]
        scores[pair % 2, t] = (both - chance * jnp.sum(both, axis=0, keepdims=True)).astype(LOW)

    def gather(i):
        (pair, t), (even, odd) = steps[i], parts(steps[i][0])
        at, cols = slice(pair * 128, pair * 128 + 128), slice(t * 128, (t + 1) * 128)
        part = product(turned_key[at, :], scores[pair % 2, t]) * SCALING
        turned_query[even, cols] = part[:64, :128].astype(LOW)
        turned_query[odd, cols] = part[64:, 128:].astype(LOW)
        for source, target in ((scaled_query, down_query), (mixed, down_mixed)):
            tile = source[cols, at]
            target[t * 256 : t * 256 + 128, :] = tile * low_half
            target[t * 256 + 128 : t * 256 + 256, :] = tile * high_half
        if t == tiles - 1:
            o_key[:, at] = sum(
                product(scores[pair % 2, t], down_query[t * 256 : (t + 1) * 256, :]) for t in range(tiles)
            ).astype(LOW)
            o_value[:, at] = sum(
                product(v_weights[pair, t], down_mixed[t * 256 : (t + 1) * 256, :]) for t in range(tiles)
            ).astype(LOW)

    spread(0)
    for i in range(len(steps)):
        if i + 1 < len(steps):
            spread(i + 1)
        weigh(i)
        if i > 0:
            gather(i - 1)
    gather(len(steps) - 1)
    for n in range(3):
        o_query[:, n * 256 : (n + 1) * 256] = turned_query[n * 256 : (n + 1) * 256, :].T
    o_sums[...] = jnp.zeros_like(o_sums)
    o_sums[0:1, :] = whole(fold(o_query[...].astype(F32)))
    o_sums[1:2, :] = whole(fold(o_value[...].astype(F32)))


def attention_grad(mixed, value, key, scaled_query, weights):
    count, total = value.shape[0], mixed.shape[0]
    return pl.pallas_call(
        attention_kernel,
        out_shape=[
            jax.ShapeDtypeStruct((total, D), LOW),
            jax.ShapeDtypeStruct((count, D), LOW),
            jax.ShapeDtypeStruct((count, D), LOW),
            jax.ShapeDtypeStruct((8, D), F32),
        ],
        in_specs=[vmem()] * 4 + [hbm()],
        out_specs=[vmem()] * 4,
        scratch_shapes=[
            pltpu.VMEM(weights.shape, LOW),
            pltpu.SemaphoreType.DMA((PAIRS,)),
            pltpu.VMEM((D, total), LOW),
            pltpu.VMEM((D, count), LOW),
            pltpu.VMEM((D, total), LOW),
            pltpu.VMEM((2, total // 128, count, 256), LOW),
            pltpu.VMEM((2, count, 256), F32),
            pltpu.VMEM((2, 128, 256), LOW),
            pltpu.VMEM((2 * total, 128), LOW),
            pltpu.VMEM((2 * total, 128), LOW),
        ],
        compiler_params=pltpu.CompilerParams(vmem_limit_bytes=28 << 20),
        cost_estimate=SMALL,
        name="attention_grad",
    )(mixed, value, key, scaled_query, weights)


def input_kernel(
    info, context, query, gain_one, after, grad_query, grad_key, grad_value, w_query, w_key, w_value,
    sums_one, sums_two, sum_in, sum_down, o_far, o_near, o_query, rows_grad, context_grad,
):
    count, fresh = context.shape[0], query.shape[0]
    own = count // 4
    for n in range(3):
        cols = slice(n * 256, (n + 1) * 256)
        rows_grad[:, cols] = transposed_right(grad_query[...], w_query[cols, :])
        context_grad[:, cols] = transposed_right(grad_key[...], w_key[cols, :]) + transposed_right(
            grad_value[...], w_value[cols, :]
        )
    gain = wide(gain_one)
    zero = jnp.zeros((8, D), F32)

    def pull(base, grad, carry):
        standard, inverse = standardize(base.astype(F32))
        one, two = carry
        return norm_pullback(standard, inverse, gain, grad), (one + fold(grad * standard), two + fold(grad))

    carry = (zero, zero)
    for y in range(2):
        for side, target in ((0, o_near), (1, o_far)):

            def one(i, carry):
                at = i * 64
                rows = ds((y * 2 + (info[3] ^ side)) * own + at, 64)
                grad = context_grad[rows, :]
                if side:
                    out, carry = pull(context[rows, :], grad, carry)
                else:
                    mine = info[2] == y
                    grad = grad + jnp.where(mine, rows_grad[ds(at, 64), :], 0.0)
                    out, carry = pull(context[rows, :], grad, carry)
                    out = out + jnp.where(mine, after[ds(at, 64), :], 0.0)
                target[ds(y * own + at, 64), :] = out
                return carry

            carry = lax.fori_loop(0, own // 64, one, carry)

    def rest(i, carry):
        rows = ds(i * 64, 64)
        out, carry = pull(query[rows, :], rows_grad[ds(own + i * 64, 64), :], carry)
        o_query[rows, :] = out + after[ds(own + i * 64, 64), :]
        return carry

    carry = lax.fori_loop(0, fresh // 64, rest, carry)
    for target in (o_near, o_far):
        small = target.at[2 * own :, :]
        small[0:1, :], small[1:2, :] = whole(carry[0]), whole(carry[1])
        small[2:4, :] = sums_two[:2, :]
        small[4:7, :] = sums_one[:3, :]
        small[7:8, :] = sum_down[...]
        for j in range(4):
            small[8 + j : 9 + j, :] = sum_in[:, j * D : (j + 1) * D]
        small[12:, :] = jnp.zeros((4, D), F32)


def input_grad(member, args, own, fresh, count):
    shapes = [(2 * own + 16, D), (2 * own + 16, D), (fresh, D)]
    return pl.pallas_call(
        input_kernel,
        out_shape=[jax.ShapeDtypeStruct(s, F32) for s in shapes],
        grid_spec=pltpu.PrefetchScalarGridSpec(
            num_scalar_prefetch=1,
            grid=(1,),
            in_specs=[vmem()] * len(args),
            out_specs=[vmem()] * 3,
            scratch_shapes=[pltpu.VMEM((own + fresh, D), F32), pltpu.VMEM((count, D), F32)],
        ),
        compiler_params=pltpu.CompilerParams(vmem_limit_bytes=24 << 20),
        cost_estimate=SMALL,
        name="input_grad",
    )(member, *args)


def body(
    context_in,
    query_in,
    context_seg,
    query_seg,
    attn_gain,
    attn_shift,
    w_query,
    b_query,
    w_key,
    w_value,
    b_value,
    w_out,
    b_out,
    mlp_gain,
    mlp_shift,
    w_in,
    b_in,
    w_down,
    b_down,
    context_cot,
    query_cot,
):
    count, fresh = context_in.shape[1], query_in.shape[1]
    seqs = lax.axis_size("seq")
    plan = Plan(seqs, lax.axis_size("qry"))
    own = count // 4
    total = own + fresh
    index, member = plan.member, plan.info
    context, query = context_in[0], query_in[0]
    direct = FF // seqs % 128 == 0
    turn = Turn()
    orders = ORDERS

    def setup(name, sides, pieces=1):
        return Setup(plan, orders[name], sides, pieces) if direct else None

    def part(kernel, name, plans, args, rows, lanes, turned):
        out = block_call(kernel, name, plan, plans, turn.wait(*args), rows, lanes, turned)
        turn.done(*out)
        return out

    def scatter(name, sent, kept):
        return [Scatter(plan, orders[name], sent, kept)]

    def spread(name, *products):
        return [Scatter(plan, orders[name], *plan.plain(transposed_left(*one), orders[name])) for one in products]

    core_pairs = [(q, q ^ 1) for q in range(4)]
    y_pairs = [(q, q ^ 2) for q in range(4)]

    (
        cot, context_low, rows_low, scaled_query, keys, values, weights, mixed, attended, normed_two, hidden, slope,
        *down_parts,
    ) = forward(
        plan,
        setup("down", (1, 0)),
        context,
        query,
        context_seg,
        query_seg,
        (attn_gain, attn_shift, b_query, b_value, b_out, mlp_gain, mlp_shift, b_in),
        (w_query, w_key, w_value, w_out, w_in),
        (context_cot[0], query_cot[0]),
    )
    turn.done(hidden)
    now = {"pins": []}

    def place(pair, near):
        low = plan.core == 0
        one, two = jnp.where(low, pair, near), jnp.where(low, near, pair)
        return jnp.stack([one, two], axis=1).reshape(count, D)

    def hidden_part():
        cot_now, slope_now = turn.wait(cot, slope)
        now["pre"], now["sum_in"], now["sum_down"] = hidden_grad(cot_now, w_down, slope_now)
        turn.done(now["pre"])
        now["D"] = scatter("down", down_parts[:1], down_parts[1]) if direct else spread("down", (hidden, cot))

    def in_part():
        if direct:
            *sent, kept = part(
                in_kernel, "in_grad", setup("in", (1, 0), 4), (normed_two, now["pre"]), D // seqs, D, [(D, total)]
            )
            now["I"] = scatter("in", sent, kept)
        else:
            now["I"] = spread("in", (normed_two, now["pre"]))

    def branch_part():
        (grad_pre,) = turn.wait(now["pre"])
        now["after"], now["branch"], now["mixed"], now["sums_one"] = branch_grad(
            member, context, query, attended, cot, mlp_gain, grad_pre, w_in, w_out
        )
        turn.done(now["mixed"])

    def output_part():
        (hidden_now,) = turn.wait(hidden)
        now["added"], now["query_out"] = outputs([], hidden_now, w_down, attended, query, b_down)
        turn.done(now["added"])
        now["out_far"] = lax.ppermute(now["added"], "qry", y_pairs)

    def attention_part():
        (grad_mixed,) = turn.wait(now["mixed"])
        now["gq"], now["gk"], now["gv"], now["sums_two"] = attention_grad(
            grad_mixed, values, keys, scaled_query, weights
        )
        turn.done(now["gq"])

    def square_part():
        args = (context_low, rows_low, mixed, now["gk"], now["gv"], now["gq"], now["branch"])
        if direct:
            out = square_call(plan, [setup("keys", (1, 0)), setup("rows", (1, 0))], turn.wait(*args))
            turn.done(*out)
            now["K"], now["R"] = scatter("keys", [out[0]], out[1]), scatter("rows", [out[2]], out[3])
        else:
            now["K"] = spread("keys", (context_low, now["gk"]), (context_low, now["gv"]))
            now["R"] = spread("rows", (rows_low, now["gq"]), (mixed, now["branch"]))

    def input_part():
        (grad_query,) = turn.wait(now["gq"])
        far, now["near"], now["query_grad"] = input_grad(
            member,
            (
                context, query, attn_gain, now["after"], grad_query, now["gk"], now["gv"], w_query, w_key, w_value,
                now["sums_one"], now["sums_two"], now["sum_in"], now["sum_down"],
            ),
            own,
            fresh,
            count,
        )
        turn.done(now["query_grad"])
        now["received"] = lax.ppermute(far, "qry", core_pairs)

    def context_part():
        near, received = turn.wait(now["near"], now["received"])
        now["pair"] = near + received
        turn.done(now["pair"])
        now["pair_far"] = lax.ppermute(now["pair"], "qry", y_pairs)

    def small_start():
        bit = now["bit"]
        if bit < plan.bits:
            now["small_far"] = lax.ppermute(now["small"], "seq", [(s, s ^ (1 << bit)) for s in range(seqs)])

    def gradient_part():
        pair, far = turn.wait(now["pair"], now["pair_far"])
        now["grad_pair"] = (pair[: 2 * own] + far[: 2 * own]).reshape(2, own, D)
        now["small"], now["bit"] = pair[2 * own :] + far[2 * own :], 0
        turn.done(now["grad_pair"], now["small"])
        now["grad_near"] = lax.ppermute(now["grad_pair"], "qry", core_pairs)
        small_start()

    def small_part():
        small, far = turn.wait(now["small"], now["small_far"])
        now["small"] = add_small(now["pins"], small, far)
        now["pins"] = []
        now["bit"] += 1
        turn.done(now["small"])
        small_start()

    def pair_part():
        added, far = turn.wait(now["added"], now["out_far"])
        first = plan.y == 0
        now["out_pair"] = jnp.stack([jnp.where(first, added, far), jnp.where(first, far, added)])
        turn.done(now["out_pair"])
        now["out_near"] = lax.ppermute(now["out_pair"], "qry", core_pairs)

    def context_grad_part():
        now["context_grad"] = place(now["grad_pair"], now["grad_near"])
        now["pins"].append(now["context_grad"])

    def context_out_part():
        now["context_out"] = (context.astype(F32) + place(now["out_pair"], now["out_near"])).astype(LOW)
        now["pins"].append(now["context_out"])

    def touch(name):
        def act():
            (now[name],) = turn.wait(now[name])
            turn.done(now[name])

        return act

    def touch_group(name):
        def act():
            for one in now[name]:
                one.touch(turn)

        return act

    def step(name):
        return lambda: [one.step(turn) for one in now[name]]

    def finish(name):
        def act():
            now["done" + name] = [one.finish(turn) for one in now[name]]
            now["pins"] += now["done" + name]

        return act

    acts = {
        "hid": hidden_part, "in": in_part, "br": branch_part, "out": output_part, "att": attention_part,
        "sq": square_part, "inp": input_part, "ctx": context_part, "grad": gradient_part, "sm": small_part,
        "op": pair_part, "cg": context_grad_part, "co": context_out_part, "t_far": touch("out_far"), "t_near": touch("out_near"), "t_grad": touch("grad_near"),
    }
    for name in "DIKR":
        acts |= {name: step(name), "t" + name: touch_group(name), "f" + name: finish(name)}
    for name in SCRIPT:
        acts[name]()
    while now["bit"] < plan.bits:
        small_part()
    small, query_out, query_grad = now["small"], now["query_out"], now["query_grad"]
    (grad_down,), (grad_in,), first, second = now["doneD"], now["doneI"], now["doneK"], now["doneR"]
    if direct:
        grad_down = grad_down.T
        grad_w_key, grad_w_value = first[0][:, :192], first[0][:, 192:]
        grad_w_query, grad_w_out = second[0][:, :192], second[0][:, 192:]
    else:
        (grad_w_key, grad_w_value), (grad_w_query, grad_w_out) = first, second

    context_grad, context_out = now["context_grad"], now["context_out"]
    return (
        context_out[None],
        query_out[None],
        context_grad[None],
        query_grad[None],
        small[0],
        small[1],
        grad_w_query,
        small[2],
        grad_w_key,
        grad_w_value,
        small[3],
        grad_w_out,
        small[4],
        small[5],
        small[6],
        grad_in,
        small[8:12].reshape(-1),
        grad_down,
        small[7],
    )


def solution(mesh):
    placed = (
        P("seq", None, None),
        P("seq", "qry", None),
        P("seq", None),
        P("seq", "qry"),
        P(),
        P(),
        P(),
        P(),
        P(),
        P(),
        P(),
        P(),
        P(),
        P(),
        P(),
        P(),
        P(),
        P(),
        P(),
        P("seq", None, None),
        P("seq", "qry", None),
    )
    return jax.shard_map(
        body,
        mesh=mesh,
        in_specs=placed,
        out_specs=(
            P("seq", None, None),
            P("seq", "qry", None),
            P("seq", None, None),
            P("seq", "qry", None),
            P(),
            P(),
            P("seq", "qry"),
            P(),
            P("seq", "qry"),
            P("seq", "qry"),
            P(),
            P("seq", "qry"),
            P(),
            P(),
            P(),
            P("seq", "qry"),
            P(),
            P("seq", "qry"),
            P(),
        ),
        check_vma=False,
    )
```

```python
import functools

import jax
import jax.numpy as jnp
from jax import lax
from jax.experimental import pallas as pl
from jax.experimental.pallas import tpu as pltpu
from jax.sharding import PartitionSpec as P

D = 768
HEADS = 12
HEAD_DIM = 64
FF = 3072
PAIRS = HEADS // 2

EPSILON = 1e-05
MASKED = -1e30
LOW = jnp.bfloat16
F32 = jnp.float32
SCALING = HEAD_DIM ** (-0.5)
BEND = 0.7978845608028654
CUBE = 0.044715 * BEND


def standardize(values):
    center = values - jnp.mean(values, axis=-1, keepdims=True)
    spread = jnp.mean(center * center, axis=-1, keepdims=True)
    inverse = lax.rsqrt(spread + EPSILON)
    return center * inverse, inverse


def norm_pullback(standard, inverse, gain, grad):
    scaled = grad * gain
    first = jnp.mean(scaled, axis=-1, keepdims=True)
    second = jnp.mean(scaled * standard, axis=-1, keepdims=True)
    return inverse * (scaled - first - standard * second)


def product(left, right):
    return jnp.dot(left, right, preferred_element_type=F32)


def transposed_left(left, right):
    return lax.dot_general(left, right, (((0,), (0,)), ((), ())), preferred_element_type=F32)


def transposed_right(left, right):
    return lax.dot_general(left, right, (((1,), (1,)), ((), ())), preferred_element_type=F32)


def wide(ref):
    return ref[...].astype(F32).reshape(1, -1)


def ds(start, size):
    return pl.ds(pl.multiple_of(start, size), size)


def fold(values):
    return jnp.sum(values.reshape(values.shape[0] // 8, 8, values.shape[1]), axis=0)


def whole(values):
    return jnp.sum(values, axis=0, keepdims=True)


def vmem():
    return pl.BlockSpec(memory_space=pltpu.VMEM)


def hbm():
    return pl.BlockSpec(memory_space=pltpu.HBM)


SMALL = pl.CostEstimate(flops=0, bytes_accessed=0, transcendentals=0)


LIMIT = 28

ORDERS = {
    "down": ("lyxh", "xlyh"),
    "in": ("yhxl", "xlyh"),
    "keys": ("xlyh", "lxyh"),
    "rows": ("yxlh", "xyhl"),
}
SCRIPT = (
    "hid", "D", "in", "br", "I", "att", "D", "sq", "inp", "tI", "K", "R", "I", "D", "ctx", "K", "R",
    "D", "out", "R", "I", "K", "grad", "fD", "sm", "I", "op", "cg", "sm", "R", "K", "co", "sm", "fI",
    "fR", "fK",
)


def after(tokens, kernel, specs, args):
    at = len(args)

    def ordered(*refs):
        return kernel(*refs[:at], *refs[at + len(tokens) :])

    return ordered, list(specs) + [hbm()] * len(tokens), tuple(args) + tuple(tokens)


class Copies:
    def __init__(self, sems):
        self.sems, self.all = sems, []

    def start(self, source, target):
        copy = pltpu.make_async_copy(source, target, self.sems.at[len(self.all)])
        copy.start()
        self.all.append(copy)
        return copy

    def wait(self):
        for copy in self.all:
            copy.wait()


class Plan:
    def __init__(self, seqs, members):
        assert members == 4 and seqs & (seqs - 1) == 0 and seqs >= 8
        self.seqs = seqs
        self.bits = seqs.bit_length() - 1
        self.stages = self.bits + 1
        self.blocks = 2 * seqs
        self.s = lax.axis_index("seq")
        self.member = lax.axis_index("qry")
        self.y, self.core = self.member // 2, self.member % 2
        self.info = jnp.stack([self.member, self.s, self.y, self.core]).astype(jnp.int32)

    def order(self, letters):
        return ["y" if letter == "y" else "xlh".index(letter) for letter in letters] + list(range(3, self.bits))

    def pairs(self, orders, step):
        out = []
        for s in range(self.seqs):
            for y in range(2):
                for core in range(2):
                    bit = self.order(orders[core])[step]
                    to = (s, y ^ 1) if bit == "y" else (s ^ (1 << bit), y)
                    out.append((s * 4 + y * 2 + core, to[0] * 4 + to[1] * 2 + core))
        return out

    def plain(self, grad, orders):
        rows, columns = grad.shape
        tail = (rows // self.seqs, columns // 4)
        parts = grad.reshape(self.seqs, tail[0], 2, 2, tail[1]).transpose(3, 0, 2, 1, 4)
        parts = parts.reshape((2,) + (2,) * self.stages + tail)
        own = {bit: (self.s >> bit) & 1 for bit in range(self.bits)} | {"y": self.y}
        axis = {bit: self.bits - bit for bit in range(self.bits)} | {"y": self.stages}
        for bit in own:
            parts = jnp.where(own[bit] == 1, jnp.flip(parts, axis[bit]), parts)
        both = [
            parts[core].transpose(*[axis[bit] - 1 for bit in self.order(orders[core])], self.stages, self.stages + 1)
            for core in range(2)
        ]
        parts = jnp.stack(both).reshape(2, self.blocks, *tail)
        kept = lax.dynamic_index_in_dim(parts, self.core, 0, keepdims=False)
        sent = lax.dynamic_index_in_dim(parts, 1 - self.core, 0, keepdims=False)
        return [sent], kept


def place_of(order, info, s, y):
    place = 0
    for step, bit in enumerate(order):
        one = (info[2] ^ y) if bit == "y" else ((info[1] ^ s) >> bit) & 1
        place = place + (one << (len(order) - 1 - step))
    return place


class Scatter:
    def __init__(self, plan, orders, sent, kept):
        self.plan, self.orders, self.stage = plan, orders, 0
        pairs = [(q, q ^ 1) for q in range(4)]
        self.terms = [kept] + [lax.ppermute(piece, "qry", pairs) for piece in sent]
        self.pieces = len(sent)

    def step(self, turn):
        plan = self.plan
        if self.stage == plan.stages:
            return
        self.terms = turn.wait(*self.terms)
        half = plan.blocks >> (self.stage + 1)
        leaving = self.sum(half, 2 * half)
        turn.done(leaving)
        self.terms = self.terms + [lax.ppermute(leaving, ("seq", "qry"), plan.pairs(self.orders, self.stage))]
        self.stage += 1

    def touch(self, turn):
        self.terms = turn.wait(*self.terms)
        turn.done(self.terms[-1])

    def sum(self, low, high):
        size = self.plan.blocks // self.pieces
        span = [self.terms[1 + i] for i in range(low // size, -(-high // size))]
        near = span[0][low % size : low % size + high - low] if len(span) == 1 else jnp.concatenate(span, axis=0)
        return functools.reduce(lambda a, b: a + b, [t[low:high] for t in self.terms[1 + self.pieces :]], self.terms[0][low:high] + near)

    def finish(self, turn):
        while self.stage < self.plan.stages:
            self.step(turn)
        self.terms = turn.wait(*self.terms)
        out = self.sum(0, 1)[0]
        turn.done(out)
        return out


class Turn:
    def __init__(self):
        self.last = []

    def wait(self, *values):
        if self.last:
            out = lax.optimization_barrier((*values, *self.last))
            values = out[: len(values)]
        return list(values)

    def done(self, *values):
        self.last = list(values)


def pick(ref, y, half):
    low = ref[:, y * 384 : y * 384 + 192]
    high = ref[:, y * 384 + 192 : y * 384 + 384]
    return jnp.where(half == 0, low, high)


def in_kernel(setup, info, normed, grad, *rest):
    seqs, outs, (turned, stage, sems) = setup.seqs, rest[: setup.outs], rest[setup.outs :]
    turned[...] = normed[...].T
    height = D // seqs
    leaves = []
    for side, half in setup.halves(info):
        leave = Blocks(setup, side, outs, sems)
        for y in range(2):
            start = pl.multiple_of((y * 2 + half) * D, 128)
            for n in range(3):
                part = product(turned[...], grad[:, pl.ds(pl.multiple_of(start + n * 256, 128), 256)])
                for s in range(seqs):
                    stage[leave.at(s, y), :, n * 256 : (n + 1) * 256] = part[s * height : (s + 1) * height]
            for s in range(seqs):
                leave.start(stage, leave.at(s, y), setup.place(half, info, s, y))
        leaves.append(leave)
    for leave in leaves:
        leave.wait(stage)


def square_kernel(setups, info, normed_context, normed, mixed, gk, gv, gq, ga, *rest):
    outs, (turned_c, turned_a, turned_o, *more) = rest[:4], rest[4:]
    turned_c[...] = normed_context[...].T
    turned_a[...] = normed[...].T
    turned_o[...] = mixed[...].T
    height = D // setups[0].seqs
    leaves = []
    for side in range(2):
        for which, setup in enumerate(setups):
            _, half = setup.halves(info)[side]
            stage, sems = more[2 * which : 2 * which + 2]
            leave = Blocks(setup, side, outs[2 * which : 2 * which + 2], sems)
            for y in range(2):
                if which == 0:
                    part = product(turned_c[...], jnp.concatenate([pick(gk, y, half), pick(gv, y, half)], axis=1))
                else:
                    part = jnp.concatenate(
                        [product(turned_a[...], pick(gq, y, half)), product(turned_o[...], pick(ga, y, half))], axis=1
                    )
                for s in range(setup.seqs):
                    stage[leave.at(s, y)] = part[s * height : (s + 1) * height]
                    leave.start(stage, leave.at(s, y), setup.place(half, info, s, y))
            leaves.append((leave, stage))
    for leave, stage in leaves:
        leave.wait(stage)


def square_call(plan, setups, args):
    blocks = plan.blocks
    rows = D // plan.seqs
    return pl.pallas_call(
        functools.partial(square_kernel, setups),
        out_shape=[pltpu.HBM((blocks, rows, 384), F32)] * 4,
        grid_spec=pltpu.PrefetchScalarGridSpec(
            num_scalar_prefetch=1,
            grid=(1,),
            in_specs=[vmem()] * len(args),
            out_specs=[hbm()] * 4,
            scratch_shapes=[pltpu.VMEM((D, a.shape[0]), LOW) for a in args[:3]]
            + [pltpu.VMEM((2 * blocks, rows, 384), F32), pltpu.SemaphoreType.DMA((2 * blocks,))] * 2,
        ),
        compiler_params=pltpu.CompilerParams(vmem_limit_bytes=LIMIT << 20),
        cost_estimate=SMALL,
        name="square_grad",
    )(plan.info, *args)


class Setup:
    def __init__(self, plan, orders, sides, pieces):
        self.seqs, self.sides, self.pieces = plan.seqs, sides, pieces
        self.orders = [plan.order(letters) for letters in orders]
        self.blocks = plan.blocks
        self.counts = [pieces if side else 1 for side in sides]
        self.outs = sum(self.counts)

    def halves(self, info):
        return [(i, info[3] ^ side) for i, side in enumerate(self.sides)]

    def place(self, half, info, s, y):
        one, two = [place_of(order, info, s, y) for order in self.orders]
        return jnp.where(half == 0, one, two)


class Blocks:
    def __init__(self, setup, side, outs, sems):
        before = sum(setup.counts[:side])
        self.outs, self.sems, self.all = outs[before : before + setup.counts[side]], sems, []
        self.first, self.seqs = side * setup.blocks, setup.seqs

    def at(self, s, y):
        return self.first + s * 2 + y

    def each(self, stage, at, place, act):
        size = self.outs[0].shape[0]
        if len(self.outs) == 1:
            act(pltpu.make_async_copy(stage.at[at], self.outs[0].at[place], self.sems.at[at]))
            return
        for i, out in enumerate(self.outs):

            @pl.when((place >= i * size) & (place < (i + 1) * size))
            def _():
                act(pltpu.make_async_copy(stage.at[at], out.at[place - i * size], self.sems.at[at]))

    def start(self, stage, at, place):
        self.all.append((at, place))
        self.each(stage, at, place, lambda copy: copy.start())

    def wait(self, stage):
        for at, place in self.all:
            self.each(stage, at, place, lambda copy: copy.wait())


def block_call(kernel, name, plan, setup, args, rows, lanes, turned):
    blocks = plan.blocks * len(setup.sides)
    shapes = []
    for count in setup.counts:
        shapes += [pltpu.HBM((plan.blocks // count, rows, lanes), F32)] * count
    return pl.pallas_call(
        functools.partial(kernel, setup),
        out_shape=shapes,
        grid_spec=pltpu.PrefetchScalarGridSpec(
            num_scalar_prefetch=1,
            grid=(1,),
            in_specs=[vmem()] * len(args),
            out_specs=[hbm()] * len(shapes),
            scratch_shapes=[pltpu.VMEM(t, LOW) for t in turned]
            + [pltpu.VMEM((blocks, rows, lanes), F32), pltpu.SemaphoreType.DMA((blocks,))],
        ),
        compiler_params=pltpu.CompilerParams(vmem_limit_bytes=LIMIT << 20),
        cost_estimate=SMALL,
        name=name,
    )(plan.info, *args)


def forward_kernel(
    setup, info, context, query, context_seg, query_seg, gain_one, shift_one, b_query, b_value, b_out, gain_two, shift_two, b_in,
    w_query, w_key, w_value, w_out, w_in, context_cot, query_cot,
    *rest,
):
    names = 12
    outs, rest = rest[:names], rest[names:]
    o_cot, o_context, o_rows, o_query, o_key, o_value, o_weights, o_mixed, o_attended, o_normed, o_hidden, o_slope = outs
    if setup:
        o_down, rest = rest[:2], rest[2:]
    v_wq, v_wk, v_wv, v_wo, v_win, sem_in, *rest = rest
    scratch, rest = rest[:names], rest[names:]
    s_cot, s_context, s_rows, s_query, s_key, s_value, s_weights, s_mixed, s_attended, s_normed, s_hidden, s_slope = scratch
    turned_query, turned_value, turned_mixed, bias, diag, scores, ahead, sem_out, *rest = rest
    if setup:
        turned_cot, stage, sem_down = rest
    count, fresh = context.shape[0], query.shape[0]
    total = s_rows.shape[0]
    own = total - fresh
    tiles = total // 128
    arrive = Copies(sem_in)
    loads = [
        arrive.start(source, target)
        for source, target in [
            (w_query, v_wq),
            (w_key, v_wk),
            (w_value, v_wv),
            (w_out, v_wo),
            (w_in, v_win),
            (context_cot.at[ds(info[0] * own, own), :], s_cot.at[:own, :]),
            (query_cot, s_cot.at[own:, :]),
        ]
    ]
    leave = Copies(sem_out)
    send = leave.start
    gain, shift = wide(gain_one), wide(shift_one)

    def normalize(source, target, at, step):
        def one(i, carry):
            rows = pl.ds(pl.multiple_of(i * step, step), step)
            standard, _ = standardize(source[rows, :].astype(F32))
            target[pl.ds(pl.multiple_of(at + i * step, step), step), :] = (standard * gain + shift).astype(LOW)
            return carry
        lax.fori_loop(0, source.shape[0] // step, one, 0)

    normalize(context, s_context, 0, 64)
    normalize(query, s_rows, own, 64)
    s_rows[:own, :] = s_context[pl.ds(pl.multiple_of(info[0] * own, own), own), :]
    send(s_context, o_context)
    send(s_rows, o_rows)

    keys = jnp.broadcast_to(context_seg[...].astype(F32), (128, count)).T
    for t in range(tiles):
        if t * 128 < own:
            rows = context_seg[:, pl.ds(pl.multiple_of(info[0] * own + t * 128, 128), 128)]
        else:
            rows = query_seg[:, t * 128 - own : t * 128 - own + 128]
        bias[:, t * 128 : (t + 1) * 128] = jnp.where(keys == rows.astype(F32), 0.0, MASKED)

    loads[0].wait()
    for n in range(3):
        cols = slice(n * 256, (n + 1) * 256)
        part = product(s_rows[...], v_wq[:, cols]) + b_query[cols].astype(F32).reshape(1, -1)
        part = (part.astype(LOW) * jnp.asarray(SCALING, LOW))
        s_query[:, cols] = part
        turned_query[cols, :] = part.T
    send(s_query, o_query)
    loads[1].wait()
    for n in range(3):
        cols = slice(n * 256, (n + 1) * 256)
        s_key[:, cols] = product(s_context[...], v_wk[:, cols]).astype(LOW)
    send(s_key, o_key)
    loads[2].wait()
    for n in range(3):
        cols = slice(n * 256, (n + 1) * 256)
        part = (product(s_context[...], v_wv[:, cols]) + b_value[cols].astype(F32).reshape(1, -1)).astype(LOW)
        s_value[:, cols] = part
        turned_value[cols, :] = part.T
    send(s_value, o_value)
    loads[5].wait()
    loads[6].wait()
    send(s_cot, o_cot)

    diag[...] = jnp.zeros_like(diag)

    steps = [(pair, t) for pair in range(PAIRS) for t in range(tiles)]

    def parts(pair):
        return slice(pair * 128, pair * 128 + 64), slice(pair * 128 + 64, pair * 128 + 128)

    def score(i):
        (pair, t), (even, odd) = steps[i], parts(steps[i][0])
        diag[i % 2, :64, :128] = turned_query[even, t * 128 : (t + 1) * 128]
        diag[i % 2, 64:, 128:] = turned_query[odd, t * 128 : (t + 1) * 128]
        scores[i % 2] = product(s_key[:, pair * 128 : pair * 128 + 128], diag[i % 2])

    def weigh(i):
        pair, t = steps[i]
        for side in range(2):
            lanes = slice(side * 128, (side + 1) * 128)
            part = scores[i % 2, :, lanes] + bias[:, t * 128 : (t + 1) * 128]
            raised = jnp.exp(part - jnp.max(part, axis=0, keepdims=True))
            scale = 1.0 / jnp.sum(raised, axis=0, keepdims=True)
            s_weights[pair, t, :, lanes] = (raised * scale).astype(LOW)

    def mix(i):
        (pair, t), (even, odd) = steps[i], parts(steps[i][0])
        both = product(turned_value[pair * 128 : pair * 128 + 128, :], s_weights[pair, t])
        turned_mixed[even, t * 128 : (t + 1) * 128] = both[:64, :128].astype(LOW)
        turned_mixed[odd, t * 128 : (t + 1) * 128] = both[64:, 128:].astype(LOW)
        if t == tiles - 1:
            send(s_weights.at[pair], o_weights.at[pair])

    score(0)
    for i in range(len(steps)):
        if i + 1 < len(steps):
            score(i + 1)
        weigh(i)
        if i > 0:
            mix(i - 1)
    mix(len(steps) - 1)
    for n in range(3):
        s_mixed[:, n * 256 : (n + 1) * 256] = turned_mixed[n * 256 : (n + 1) * 256, :].T
    send(s_mixed, o_mixed)
    loads[3].wait()
    for n in range(3):
        cols = slice(n * 256, (n + 1) * 256)
        s_attended[:, cols] = product(s_mixed[...], v_wo[:, cols]) + b_out[cols].astype(F32).reshape(1, -1)
    send(s_attended, o_attended)
    gain, shift = wide(gain_two), wide(shift_two)

    def second(i, carry):
        rows = pl.ds(pl.multiple_of(i * 64, 64), 64)

        def put(base):
            standard, _ = standardize(base.astype(F32) + s_attended[rows, :])
            s_normed[rows, :] = (standard * gain + shift).astype(LOW)

        @pl.when(i < own // 64)
        def _():
            put(context[pl.ds(pl.multiple_of(info[0] * own + i * 64, 64), 64), :])

        @pl.when(i >= own // 64)
        def _():
            put(query[pl.ds(pl.multiple_of(i * 64 - own, 64), 64), :])

        return carry

    lax.fori_loop(0, total // 64, second, 0)
    send(s_normed, o_normed)
    loads[4].wait()
    steps = FF // 256
    if setup:
        width, ready = FF // setup.seqs, 0
        downs = [Blocks(setup, side, o_down, sem_down) for side in range(2)]
        halves = [half for _, half in setup.halves(info)]
        for side, half in enumerate(halves):
            for y in range(2):
                at = (side * 2 + y) * 192
                turned_cot[at : at + 192, :] = pick(s_cot, y, half).T
    ahead[0] = product(s_normed[...], v_win[:, :256])
    for n in range(steps):
        cols = slice(n * 256, (n + 1) * 256)
        if n + 1 < steps:
            ahead[(n + 1) % 2] = product(s_normed[...], v_win[:, (n + 1) * 256 : (n + 2) * 256])
        extra = b_in[cols].astype(F32).reshape(1, -1)
        for m in range(total // 64):
            rows = slice(m * 64, (m + 1) * 64)
            h = ahead[n % 2, rows, :] + extra
            square = h * h
            t = jnp.tanh(h * (BEND + CUBE * square))
            part = 0.5 + 0.5 * t
            s_hidden[rows, cols] = (h * part).astype(LOW)
            bend = h * (BEND + 3 * CUBE * square)
            s_slope[rows, cols] = (part * (1.0 + bend * (1.0 - t))).astype(LOW)
        send(s_hidden.at[:, cols], o_hidden.at[:, cols])
        send(s_slope.at[:, cols], o_slope.at[:, cols])
        while setup and (ready + 1) * width <= (n + 1) * 256:
            part = product(turned_cot[...], s_hidden[:, ready * width : (ready + 1) * width])
            for side, half in enumerate(halves):
                for y in range(2):
                    at = downs[side].at(ready, y)
                    stage[at] = part[(side * 2 + y) * 192 : (side * 2 + y + 1) * 192]
                    downs[side].start(stage, at, setup.place(half, info, ready, y))
            ready += 1
    if setup:
        for down in downs:
            down.wait(stage)
    leave.wait()

def forward(plan, setup, context, query, context_seg, query_seg, vectors, weights, cots):
    count, fresh = context.shape[0], query.shape[0]
    own = count // 4
    total = own + fresh
    kept = [
        ((total, D), LOW),
        ((count, D), LOW),
        ((total, D), LOW),
        ((total, D), LOW),
        ((count, D), LOW),
        ((count, D), LOW),
        ((PAIRS, total // 128, count, 256), LOW),
        ((total, D), LOW),
        ((total, D), F32),
        ((total, D), LOW),
        ((total, FF), LOW),
        ((total, FF), LOW),
    ]
    block = (plan.blocks, 192, FF // plan.seqs)
    return pl.pallas_call(
        functools.partial(forward_kernel, setup),
        out_shape=[jax.ShapeDtypeStruct(*s) for s in kept] + ([pltpu.HBM(block, F32)] * 2 if setup else []),
        grid_spec=pltpu.PrefetchScalarGridSpec(
            num_scalar_prefetch=1,
            grid=(1,),
            in_specs=[vmem()] * 12 + [hbm()] * 7,
            out_specs=[hbm()] * (len(kept) + 2 * bool(setup)),
            scratch_shapes=[pltpu.VMEM((D, D), LOW)] * 4
            + [pltpu.VMEM((D, FF), LOW), pltpu.SemaphoreType.DMA((7,))]
            + [pltpu.VMEM(*s) for s in kept]
            + [
                pltpu.VMEM((D, total), LOW),
                pltpu.VMEM((D, count), LOW),
                pltpu.VMEM((D, total), LOW),
                pltpu.VMEM((count, total), F32),
                pltpu.VMEM((2, 128, 256), LOW),
                pltpu.VMEM((2, count, 256), F32),
                pltpu.VMEM((2, total, 256), F32),
                pltpu.SemaphoreType.DMA((9 + PAIRS + 2 * FF // 256,)),
            ]
            + (
                [
                    pltpu.VMEM((D, total), LOW),
                    pltpu.VMEM((2 * block[0], *block[1:]), F32),
                    pltpu.SemaphoreType.DMA((2 * plan.blocks,)),
                ]
                if setup
                else []
            ),
        ),
        compiler_params=pltpu.CompilerParams(vmem_limit_bytes=58 << 20),
        cost_estimate=SMALL,
        name="forward",
    )(plan.info, context, query, context_seg, query_seg, *vectors, *weights, *cots)


def hidden_kernel(cot, w_down, slope, out, sum_in, sum_down):
    for n in range(w_down.shape[0] // 256):
        cols = slice(n * 256, (n + 1) * 256)
        out[:, cols] = (transposed_right(cot[...], w_down[cols, :]) * slope[:, cols].astype(F32)).astype(LOW)
    sum_in[...] = whole(fold(out[...].astype(F32)))

    @pl.when(pl.program_id(0) == 0)
    def _():
        sum_down[...] = whole(fold(cot[...].astype(F32)))


def hidden_grad(cot, w_down, slope):
    total, step = cot.shape[0], 768
    return pl.pallas_call(
        hidden_kernel,
        out_shape=[
            jax.ShapeDtypeStruct((total, FF), LOW),
            jax.ShapeDtypeStruct((1, FF), F32),
            jax.ShapeDtypeStruct((1, D), F32),
        ],
        grid=(FF // step,),
        in_specs=[
            pl.BlockSpec((total, D), lambda i: (0, 0)),
            pl.BlockSpec((step, D), lambda i: (i, 0)),
            pl.BlockSpec((total, step), lambda i: (0, i)),
        ],
        out_specs=[
            pl.BlockSpec((total, step), lambda i: (0, i)),
            pl.BlockSpec((1, step), lambda i: (0, i)),
            pl.BlockSpec((1, D), lambda i: (0, 0)),
        ],
        compiler_params=pltpu.CompilerParams(vmem_limit_bytes=16 << 20),
        cost_estimate=SMALL,
        name="hidden_grad",
    )(cot, w_down, slope)


def small_kernel(left, right, out):
    out[...] = left[...] + right[...]


def add_small(tokens, left, right):
    kernel, specs, args = after(tokens, small_kernel, [vmem()] * 2, (left, right))
    return pl.pallas_call(
        kernel,
        out_shape=jax.ShapeDtypeStruct(left.shape, F32),
        in_specs=specs,
        out_specs=vmem(),
        cost_estimate=SMALL,
        name="add_small",
    )(*args)


def output_kernel(hidden, w_down, attended, query, b_down, o_added, o_query, added):
    step, last = pl.program_id(0), pl.num_programs(0) - 1
    own = o_added.shape[0]

    @pl.when(step == 0)
    def _():
        added[...] = attended[...] + wide(b_down)

    for n in range(3):
        cols = slice(n * 256, (n + 1) * 256)
        added[:, cols] += product(hidden[...], w_down[:, cols])

    @pl.when(step == last)
    def _():
        o_added[...] = added[:own, :]
        o_query[...] = (query[...].astype(F32) + added[own:, :]).astype(LOW)


def outputs(tokens, hidden, w_down, attended, query, b_down):
    total, fresh, step = hidden.shape[0], query.shape[0], 1536
    fixed = lambda rows: pl.BlockSpec((rows, D), lambda i: (0, 0))
    specs = [
        pl.BlockSpec((total, step), lambda i: (0, i)),
        pl.BlockSpec((step, D), lambda i: (i, 0)),
        fixed(total),
        fixed(fresh),
        pl.BlockSpec((D,), lambda i: (0,)),
    ]
    kernel, specs, args = after(tokens, output_kernel, specs, (hidden, w_down, attended, query, b_down))
    return pl.pallas_call(
        kernel,
        out_shape=[
            jax.ShapeDtypeStruct((total - fresh, D), F32),
            jax.ShapeDtypeStruct((fresh, D), LOW),
        ],
        grid_spec=pltpu.PrefetchScalarGridSpec(
            num_scalar_prefetch=0,
            grid=(FF // step,),
            in_specs=specs,
            out_specs=[fixed(total - fresh), fixed(fresh)],
            scratch_shapes=[pltpu.VMEM((total, D), F32)],
        ),
        compiler_params=pltpu.CompilerParams(vmem_limit_bytes=58 << 20),
        cost_estimate=SMALL,
        name="outputs",
    )(*args)


def branch_kernel(
    info, context, query, attended, cot, gain_two, grad_pre, w_in, w_out,
    o_after, o_branch, o_mixed, o_sums,
    v_win, v_wout, sem_in, normed,
):
    total, fresh = attended.shape[0], query.shape[0]
    own = total - fresh
    arrive = Copies(sem_in)
    loads = [arrive.start(w_in.at[n * 256 : (n + 1) * 256, :], v_win.at[n * 256 : (n + 1) * 256, :]) for n in range(3)]
    last = arrive.start(w_out, v_wout)
    for n in range(3):
        cols = slice(n * 256, (n + 1) * 256)
        loads[n].wait()
        normed[:, cols] = transposed_right(grad_pre[...], v_win[cols, :])
    gain = wide(gain_two)

    def back(i, carry, base):
        rows = ds(i * 32, 32)
        standard, inverse = standardize(base.astype(F32) + attended[rows, :])
        grad = normed[rows, :]
        after = cot[rows, :].astype(F32) + norm_pullback(standard, inverse, gain, grad)
        o_after[rows, :] = after
        low = after.astype(LOW)
        o_branch[rows, :] = low
        one, two, three = carry
        return one + fold(grad * standard), two + fold(grad), three + fold(low.astype(F32))

    zero = jnp.zeros((8, D), F32)
    sums = lax.fori_loop(
        0, own // 32, lambda i, c: back(i, c, context[ds(info[0] * own + i * 32, 32), :]), (zero, zero, zero)
    )
    sums = lax.fori_loop(own // 32, total // 32, lambda i, c: back(i, c, query[ds(i * 32 - own, 32), :]), sums)
    o_sums[...] = jnp.zeros_like(o_sums)
    o_sums[0:1, :], o_sums[1:2, :], o_sums[2:3, :] = whole(sums[2]), whole(sums[0]), whole(sums[1])
    last.wait()
    for n in range(3):
        cols = slice(n * 256, (n + 1) * 256)
        o_mixed[:, cols] = transposed_right(o_branch[...], v_wout[cols, :]).astype(LOW)


def branch_grad(member, context, query, attended, cot, gain_two, grad_pre, w_in, w_out):
    total = attended.shape[0]
    return pl.pallas_call(
        branch_kernel,
        out_shape=[
            jax.ShapeDtypeStruct((total, D), F32),
            jax.ShapeDtypeStruct((total, D), LOW),
            jax.ShapeDtypeStruct((total, D), LOW),
            jax.ShapeDtypeStruct((8, D), F32),
        ],
        grid_spec=pltpu.PrefetchScalarGridSpec(
            num_scalar_prefetch=1,
            grid=(1,),
            in_specs=[vmem()] * 6 + [hbm()] * 2,
            out_specs=[vmem()] * 4,
            scratch_shapes=[
                pltpu.VMEM((D, FF), LOW),
                pltpu.VMEM((D, D), LOW),
                pltpu.SemaphoreType.DMA((4,)),
                pltpu.VMEM((total, D), F32),
            ],
        ),
        compiler_params=pltpu.CompilerParams(vmem_limit_bytes=28 << 20),
        cost_estimate=SMALL,
        name="branch_grad",
    )(member, context, query, attended, cot, gain_two, grad_pre, w_in, w_out)


def attention_kernel(
    mixed, value, key, scaled_query, weights, o_query, o_key, o_value, o_sums,
    v_weights, sem_in, turned_mixed, turned_key, turned_query, scores, ahead, across, down_query, down_mixed,
):
    total = mixed.shape[0]
    tiles = total // 128
    arrive = Copies(sem_in)
    loads = [arrive.start(weights.at[pair], v_weights.at[pair]) for pair in range(PAIRS)]
    for n in range(3):
        cols = slice(n * 256, (n + 1) * 256)
        turned_mixed[cols, :] = mixed[:, cols].T
        turned_key[cols, :] = key[:, cols].T
    across[...] = jnp.zeros_like(across)
    lane = lax.broadcasted_iota(jnp.int32, (1, 128), 1)
    low_half = (lane < 64).astype(F32).astype(LOW)
    high_half = (lane >= 64).astype(F32).astype(LOW)
    steps = [(pair, t) for pair in range(PAIRS) for t in range(tiles)]

    def parts(pair):
        return slice(pair * 128, pair * 128 + 64), slice(pair * 128 + 64, pair * 128 + 128)

    def spread(i):
        (pair, t), (even, odd) = steps[i], parts(steps[i][0])
        across[i % 2, :64, :128] = turned_mixed[even, t * 128 : (t + 1) * 128]
        across[i % 2, 64:, 128:] = turned_mixed[odd, t * 128 : (t + 1) * 128]
        ahead[i % 2] = product(value[:, pair * 128 : pair * 128 + 128], across[i % 2])

    def weigh(i):
        pair, t = steps[i]
        if t == 0:
            loads[pair].wait()
        chance = v_weights[pair, t].astype(F32)
        both = chance * ahead[i % 2]
        scores[pair % 2, t] = (both - chance * jnp.sum(both, axis=0, keepdims=True)).astype(LOW)

    def gather(i):
        (pair, t), (even, odd) = steps[i], parts(steps[i][0])
        at, cols = slice(pair * 128, pair * 128 + 128), slice(t * 128, (t + 1) * 128)
        part = product(turned_key[at, :], scores[pair % 2, t]) * SCALING
        turned_query[even, cols] = part[:64, :128].astype(LOW)
        turned_query[odd, cols] = part[64:, 128:].astype(LOW)
        for source, target in ((scaled_query, down_query), (mixed, down_mixed)):
            tile = source[cols, at]
            target[t * 256 : t * 256 + 128, :] = tile * low_half
            target[t * 256 + 128 : t * 256 + 256, :] = tile * high_half
        if t == tiles - 1:
            o_key[:, at] = sum(
                product(scores[pair % 2, t], down_query[t * 256 : (t + 1) * 256, :]) for t in range(tiles)
            ).astype(LOW)
            o_value[:, at] = sum(
                product(v_weights[pair, t], down_mixed[t * 256 : (t + 1) * 256, :]) for t in range(tiles)
            ).astype(LOW)

    spread(0)
    for i in range(len(steps)):
        if i + 1 < len(steps):
            spread(i + 1)
        weigh(i)
        if i > 0:
            gather(i - 1)
    gather(len(steps) - 1)
    for n in range(3):
        o_query[:, n * 256 : (n + 1) * 256] = turned_query[n * 256 : (n + 1) * 256, :].T
    o_sums[...] = jnp.zeros_like(o_sums)
    o_sums[0:1, :] = whole(fold(o_query[...].astype(F32)))
    o_sums[1:2, :] = whole(fold(o_value[...].astype(F32)))


def attention_grad(mixed, value, key, scaled_query, weights):
    count, total = value.shape[0], mixed.shape[0]
    return pl.pallas_call(
        attention_kernel,
        out_shape=[
            jax.ShapeDtypeStruct((total, D), LOW),
            jax.ShapeDtypeStruct((count, D), LOW),
            jax.ShapeDtypeStruct((count, D), LOW),
            jax.ShapeDtypeStruct((8, D), F32),
        ],
        in_specs=[vmem()] * 4 + [hbm()],
        out_specs=[vmem()] * 4,
        scratch_shapes=[
            pltpu.VMEM(weights.shape, LOW),
            pltpu.SemaphoreType.DMA((PAIRS,)),
            pltpu.VMEM((D, total), LOW),
            pltpu.VMEM((D, count), LOW),
            pltpu.VMEM((D, total), LOW),
            pltpu.VMEM((2, total // 128, count, 256), LOW),
            pltpu.VMEM((2, count, 256), F32),
            pltpu.VMEM((2, 128, 256), LOW),
            pltpu.VMEM((2 * total, 128), LOW),
            pltpu.VMEM((2 * total, 128), LOW),
        ],
        compiler_params=pltpu.CompilerParams(vmem_limit_bytes=28 << 20),
        cost_estimate=SMALL,
        name="attention_grad",
    )(mixed, value, key, scaled_query, weights)


def input_kernel(
    info, context, query, gain_one, after, grad_query, grad_key, grad_value, w_query, w_key, w_value,
    sums_one, sums_two, sum_in, sum_down, o_far, o_near, o_query, rows_grad, context_grad,
):
    count, fresh = context.shape[0], query.shape[0]
    own = count // 4
    for n in range(3):
        cols = slice(n * 256, (n + 1) * 256)
        rows_grad[:, cols] = transposed_right(grad_query[...], w_query[cols, :])
        context_grad[:, cols] = transposed_right(grad_key[...], w_key[cols, :]) + transposed_right(
            grad_value[...], w_value[cols, :]
        )
    gain = wide(gain_one)
    zero = jnp.zeros((8, D), F32)

    def pull(base, grad, carry):
        standard, inverse = standardize(base.astype(F32))
        one, two = carry
        return norm_pullback(standard, inverse, gain, grad), (one + fold(grad * standard), two + fold(grad))

    carry = (zero, zero)
    for y in range(2):
        for side, target in ((0, o_near), (1, o_far)):

            def one(i, carry):
                at = i * 64
                rows = ds((y * 2 + (info[3] ^ side)) * own + at, 64)
                grad = context_grad[rows, :]
                if side:
                    out, carry = pull(context[rows, :], grad, carry)
                else:
                    mine = info[2] == y
                    grad = grad + jnp.where(mine, rows_grad[ds(at, 64), :], 0.0)
                    out, carry = pull(context[rows, :], grad, carry)
                    out = out + jnp.where(mine, after[ds(at, 64), :], 0.0)
                target[ds(y * own + at, 64), :] = out
                return carry

            carry = lax.fori_loop(0, own // 64, one, carry)

    def rest(i, carry):
        rows = ds(i * 64, 64)
        out, carry = pull(query[rows, :], rows_grad[ds(own + i * 64, 64), :], carry)
        o_query[rows, :] = out + after[ds(own + i * 64, 64), :]
        return carry

    carry = lax.fori_loop(0, fresh // 64, rest, carry)
    for target in (o_near, o_far):
        small = target.at[2 * own :, :]
        small[0:1, :], small[1:2, :] = whole(carry[0]), whole(carry[1])
        small[2:4, :] = sums_two[:2, :]
        small[4:7, :] = sums_one[:3, :]
        small[7:8, :] = sum_down[...]
        for j in range(4):
            small[8 + j : 9 + j, :] = sum_in[:, j * D : (j + 1) * D]
        small[12:, :] = jnp.zeros((4, D), F32)


def input_grad(member, args, own, fresh, count):
    shapes = [(2 * own + 16, D), (2 * own + 16, D), (fresh, D)]
    return pl.pallas_call(
        input_kernel,
        out_shape=[jax.ShapeDtypeStruct(s, F32) for s in shapes],
        grid_spec=pltpu.PrefetchScalarGridSpec(
            num_scalar_prefetch=1,
            grid=(1,),
            in_specs=[vmem()] * len(args),
            out_specs=[vmem()] * 3,
            scratch_shapes=[pltpu.VMEM((own + fresh, D), F32), pltpu.VMEM((count, D), F32)],
        ),
        compiler_params=pltpu.CompilerParams(vmem_limit_bytes=24 << 20),
        cost_estimate=SMALL,
        name="input_grad",
    )(member, *args)


def body(
    context_in,
    query_in,
    context_seg,
    query_seg,
    attn_gain,
    attn_shift,
    w_query,
    b_query,
    w_key,
    w_value,
    b_value,
    w_out,
    b_out,
    mlp_gain,
    mlp_shift,
    w_in,
    b_in,
    w_down,
    b_down,
    context_cot,
    query_cot,
):
    count, fresh = context_in.shape[1], query_in.shape[1]
    seqs = lax.axis_size("seq")
    plan = Plan(seqs, lax.axis_size("qry"))
    own = count // 4
    total = own + fresh
    index, member = plan.member, plan.info
    context, query = context_in[0], query_in[0]
    direct = FF // seqs % 128 == 0
    turn = Turn()
    orders = ORDERS

    def setup(name, sides, pieces=1):
        return Setup(plan, orders[name], sides, pieces) if direct else None

    def part(kernel, name, plans, args, rows, lanes, turned):
        out = block_call(kernel, name, plan, plans, turn.wait(*args), rows, lanes, turned)
        turn.done(*out)
        return out

    def scatter(name, sent, kept):
        return [Scatter(plan, orders[name], sent, kept)]

    def spread(name, *products):
        return [Scatter(plan, orders[name], *plan.plain(transposed_left(*one), orders[name])) for one in products]

    core_pairs = [(q, q ^ 1) for q in range(4)]
    y_pairs = [(q, q ^ 2) for q in range(4)]

    (
        cot, context_low, rows_low, scaled_query, keys, values, weights, mixed, attended, normed_two, hidden, slope,
        *down_parts,
    ) = forward(
        plan,
        setup("down", (1, 0)),
        context,
        query,
        context_seg,
        query_seg,
        (attn_gain, attn_shift, b_query, b_value, b_out, mlp_gain, mlp_shift, b_in),
        (w_query, w_key, w_value, w_out, w_in),
        (context_cot[0], query_cot[0]),
    )
    turn.done(hidden)
    now = {"pins": []}

    def place(pair, near):
        low = plan.core == 0
        one, two = jnp.where(low, pair, near), jnp.where(low, near, pair)
        return jnp.stack([one, two], axis=1).reshape(count, D)

    def hidden_part():
        cot_now, slope_now = turn.wait(cot, slope)
        now["pre"], now["sum_in"], now["sum_down"] = hidden_grad(cot_now, w_down, slope_now)
        turn.done(now["pre"])
        now["D"] = scatter("down", down_parts[:1], down_parts[1]) if direct else spread("down", (hidden, cot))

    def in_part():
        if direct:
            *sent, kept = part(
                in_kernel, "in_grad", setup("in", (1, 0), 4), (normed_two, now["pre"]), D // seqs, D, [(D, total)]
            )
            now["I"] = scatter("in", sent, kept)
        else:
            now["I"] = spread("in", (normed_two, now["pre"]))

    def branch_part():
        (grad_pre,) = turn.wait(now["pre"])
        now["after"], now["branch"], now["mixed"], now["sums_one"] = branch_grad(
            member, context, query, attended, cot, mlp_gain, grad_pre, w_in, w_out
        )
        turn.done(now["mixed"])

    def output_part():
        (hidden_now,) = turn.wait(hidden)
        now["added"], now["query_out"] = outputs([], hidden_now, w_down, attended, query, b_down)
        turn.done(now["added"])
        now["out_far"] = lax.ppermute(now["added"], "qry", y_pairs)

    def attention_part():
        (grad_mixed,) = turn.wait(now["mixed"])
        now["gq"], now["gk"], now["gv"], now["sums_two"] = attention_grad(
            grad_mixed, values, keys, scaled_query, weights
        )
        turn.done(now["gq"])

    def square_part():
        args = (context_low, rows_low, mixed, now["gk"], now["gv"], now["gq"], now["branch"])
        if direct:
            out = square_call(plan, [setup("keys", (1, 0)), setup("rows", (1, 0))], turn.wait(*args))
            turn.done(*out)
            now["K"], now["R"] = scatter("keys", [out[0]], out[1]), scatter("rows", [out[2]], out[3])
        else:
            now["K"] = spread("keys", (context_low, now["gk"]), (context_low, now["gv"]))
            now["R"] = spread("rows", (rows_low, now["gq"]), (mixed, now["branch"]))

    def input_part():
        (grad_query,) = turn.wait(now["gq"])
        far, now["near"], now["query_grad"] = input_grad(
            member,
            (
                context, query, attn_gain, now["after"], grad_query, now["gk"], now["gv"], w_query, w_key, w_value,
                now["sums_one"], now["sums_two"], now["sum_in"], now["sum_down"],
            ),
            own,
            fresh,
            count,
        )
        turn.done(now["query_grad"])
        now["received"] = lax.ppermute(far, "qry", core_pairs)

    def context_part():
        near, received = turn.wait(now["near"], now["received"])
        now["pair"] = near + received
        turn.done(now["pair"])
        now["pair_far"] = lax.ppermute(now["pair"], "qry", y_pairs)

    def small_start():
        bit = now["bit"]
        if bit < plan.bits:
            now["small_far"] = lax.ppermute(now["small"], "seq", [(s, s ^ (1 << bit)) for s in range(seqs)])

    def gradient_part():
        pair, far = turn.wait(now["pair"], now["pair_far"])
        now["grad_pair"] = (pair[: 2 * own] + far[: 2 * own]).reshape(2, own, D)
        now["small"], now["bit"] = pair[2 * own :] + far[2 * own :], 0
        turn.done(now["grad_pair"], now["small"])
        now["grad_near"] = lax.ppermute(now["grad_pair"], "qry", core_pairs)
        small_start()

    def small_part():
        small, far = turn.wait(now["small"], now["small_far"])
        now["small"] = add_small(now["pins"], small, far)
        now["pins"] = []
        now["bit"] += 1
        turn.done(now["small"])
        small_start()

    def pair_part():
        added, far = turn.wait(now["added"], now["out_far"])
        first = plan.y == 0
        now["out_pair"] = jnp.stack([jnp.where(first, added, far), jnp.where(first, far, added)])
        turn.done(now["out_pair"])
        now["out_near"] = lax.ppermute(now["out_pair"], "qry", core_pairs)

    def context_grad_part():
        now["context_grad"] = place(now["grad_pair"], now["grad_near"])
        now["pins"].append(now["context_grad"])

    def context_out_part():
        now["context_out"] = (context.astype(F32) + place(now["out_pair"], now["out_near"])).astype(LOW)
        now["pins"].append(now["context_out"])

    def touch(name):
        def act():
            (now[name],) = turn.wait(now[name])
            turn.done(now[name])

        return act

    def touch_group(name):
        def act():
            for one in now[name]:
                one.touch(turn)

        return act

    def step(name):
        return lambda: [one.step(turn) for one in now[name]]

    def finish(name):
        def act():
            now["done" + name] = [one.finish(turn) for one in now[name]]
            now["pins"] += now["done" + name]

        return act

    acts = {
        "hid": hidden_part, "in": in_part, "br": branch_part, "out": output_part, "att": attention_part,
        "sq": square_part, "inp": input_part, "ctx": context_part, "grad": gradient_part, "sm": small_part,
        "op": pair_part, "cg": context_grad_part, "co": context_out_part, "t_far": touch("out_far"), "t_near": touch("out_near"), "t_grad": touch("grad_near"),
    }
    for name in "DIKR":
        acts |= {name: step(name), "t" + name: touch_group(name), "f" + name: finish(name)}
    for name in SCRIPT:
        acts[name]()
    while now["bit"] < plan.bits:
        small_part()
    small, query_out, query_grad = now["small"], now["query_out"], now["query_grad"]
    (grad_down,), (grad_in,), first, second = now["doneD"], now["doneI"], now["doneK"], now["doneR"]
    if direct:
        grad_down = grad_down.T
        grad_w_key, grad_w_value = first[0][:, :192], first[0][:, 192:]
        grad_w_query, grad_w_out = second[0][:, :192], second[0][:, 192:]
    else:
        (grad_w_key, grad_w_value), (grad_w_query, grad_w_out) = first, second

    context_grad, context_out = now["context_grad"], now["context_out"]
    return (
        context_out[None],
        query_out[None],
        context_grad[None],
        query_grad[None],
        small[0],
        small[1],
        grad_w_query,
        small[2],
        grad_w_key,
        grad_w_value,
        small[3],
        grad_w_out,
        small[4],
        small[5],
        small[6],
        grad_in,
        small[8:12].reshape(-1),
        grad_down,
        small[7],
    )


def solution(mesh):
    placed = (
        P("seq", None, None),
        P("seq", "qry", None),
        P("seq", None),
        P("seq", "qry"),
        P(),
        P(),
        P(),
        P(),
        P(),
        P(),
        P(),
        P(),
        P(),
        P(),
        P(),
        P(),
        P(),
        P(),
        P(),
        P("seq", None, None),
        P("seq", "qry", None),
    )
    return jax.shard_map(
        body,
        mesh=mesh,
        in_specs=placed,
        out_specs=(
            P("seq", None, None),
            P("seq", "qry", None),
            P("seq", None, None),
            P("seq", "qry", None),
            P(),
            P(),
            P("seq", "qry"),
            P(),
            P("seq", "qry"),
            P("seq", "qry"),
            P(),
            P("seq", "qry"),
            P(),
            P(),
            P(),
            P("seq", "qry"),
            P(),
            P("seq", "qry"),
            P(),
        ),
        check_vma=False,
    )
```
